128 devices in a mesh: row: 32 (over x, z, core), col: 4 (over y).
Axes of the slice: x: 4, y: 4, z: 4, core: 2. Of those that a mesh axis runs over, the one named last changes fastest.
Arguments:
- front: float32 [3, 32, 24, 4, 128, 128], P(None, 'row', None, 'col'), may hold values from -6 to 6
- child_tiles: float32 [8192, 128, 128], P(('row', 'col')), may hold values from -6 to 6
- tile_dest: int32 [8192, 1], P(('row', 'col')), may hold values from 0 to 127; in each aligned block of 64 rows (0 to 63, 64 to 127, ...) no two rows name the same one
- tile_slot: int32 [8192], P(('row', 'col')), may hold values from 0 to 71
- tile_count: int32 [128], P(('row', 'col')), may hold values from 48 to 64, as said below
- diag_inverses: float32 [2, 256, 256], replicated, as said below
Outputs:
- factored: float32 [3, 32, 24, 4, 128, 128], P(None, 'row', None, 'col')
The draws below stay inside these ranges and needn't reach their ends.
Inputs may be any that keep to these rules, and one draw needn't show every extreme that they name: Among the 64 slots of one device, no two name the same device in tile_dest, live or not; every device is named by some slot. `tile_count`: some device has all 64 slots live. `diag_inverses`: each matrix is upper triangular with a positive diagonal; it is given as it is and need not match any diagonal block of the front.
All inputs are finite; a program needn't handle non-finite values.
Results may differ from the reference program's by a relative error of at most 0.000068.
Values sent between devices are 32-bit elements; how exact they have to be, the bound alone decides.
A program may use at most 128 MiB of HBM per device.

```python
import math
import jax
import jax.numpy as jnp
import numpy as np
from jax import lax

N = 12288
TILE = 128
PANEL = 256
RT = 3
CT = 24
KT = 64
N_ROW = 32
N_COL = 4
DEVICES = 128


def draw_tile_count(key, part):
    first_key, second_key = jax.random.split(jax.random.fold_in(key, 11))
    counts = jax.random.randint(first_key, (DEVICES,), KT - KT // 4, KT + 1).astype(jnp.int32)
    where_full = jax.random.randint(second_key, (), 0, DEVICES)
    full_mask = jnp.arange(DEVICES, dtype=jnp.int32) == where_full
    return jnp.where(full_mask, jnp.int32(KT), counts).astype(jnp.int32)


def draw_diag_inverses(key, part):
    first_key, second_key = jax.random.split(jax.random.fold_in(key, 23))
    upper_part = jnp.clip(jax.random.normal(first_key, (2, PANEL, PANEL), jnp.float32), -4.0, 4.0)
    upper_part = upper_part * (0.25 / math.sqrt(PANEL))
    diagonal = jnp.exp(jax.random.uniform(second_key, (2, PANEL), jnp.float32, math.log(0.08), math.log(0.3)))
    eye_table = jnp.eye(PANEL, dtype=jnp.float32)
    return (jnp.triu(upper_part, 1) + diagonal[:, :, None] * eye_table[None]).astype(jnp.float32)


def touch_ends(result, own_key, smallest, top_value):
    longest = result.shape.index(max(result.shape))
    spots = []
    for shift in (0, 1):
        where = [jax.random.randint(jax.random.fold_in(own_key, axis), (), 0, length) for axis, length in enumerate(result.shape)]
        where[longest] = (where[longest] + shift) % result.shape[longest]
        spots.append(tuple(where))
    return result.at[spots[0]].set(smallest).at[spots[1]].set(top_value)


def levels(stream_key, dims, shards, low, largest):
    def one(dim, blocks):
        steps = jax.random.uniform(jax.random.fold_in(jax.random.fold_in(stream_key, 6), dim), (blocks,), jnp.float32, low / len(shards), largest / len(shards))
        return jnp.repeat(jnp.exp(steps), dims[dim] // blocks).reshape((-1,) + (1,) * (len(dims) - dim - 1))

    gain = one(*shards[0])
    for cut in shards[1:]:
        gain = gain * one(*cut)
    return gain


def assign_block(own_key, own, number, rows, number_of, top, limit, skew):
    ranking = jax.random.permutation(own_key, number_of)
    crowded, usual = load_shares(number_of, rows * top, limit, skew, True), load_shares(number_of, rows * top, limit, skew, False)
    places = jnp.arange(number_of)

    def named(lengths, rotation):
        used = int((lengths > 0).sum())
        fixed = max(1, used // 4)
        moved = fixed + (places - fixed + rotation * (used - fixed)) % max(1, number_of - fixed)
        return jnp.zeros((number_of,), jnp.int32).at[ranking[jnp.where(places < fixed, places, moved)]].set(jnp.asarray(lengths, jnp.int32))

    lengths = jnp.where(number % 4 == 0, named(crowded, number // 4), named(usual, number - number // 4 - 1))
    mixed = jax.random.permutation(jax.random.fold_in(own, 3), number_of)
    donor, taker = mixed[0:number_of // 2 * 2:2], mixed[1:number_of // 2 * 2:2]
    room = jnp.minimum(lengths[donor] - 1, limit - lengths[taker]) // 2
    room = jnp.where((donor == ranking[0]) | (taker == ranking[0]) | (lengths[taker] == 0), 0, jnp.maximum(room, 0))
    moved = jax.random.randint(jax.random.fold_in(own, 4), (number_of // 2,), 0, 1 << 20) % (room + 1)
    lengths = lengths.at[donor].add(-moved).at[taker].add(moved)
    members = jnp.searchsorted(jnp.cumsum(lengths), jnp.arange(rows * top), side="right").astype(jnp.int32)
    grid = members.reshape(top, rows).T
    grid = grid[jax.random.permutation(jax.random.fold_in(own, 1), rows)]
    rotation = jax.random.randint(jax.random.fold_in(own, 2), (rows, 1), 0, top)
    return jnp.take_along_axis(grid, (jnp.arange(top)[None, :] + rotation) % top, axis=1)


def load_shares(count, total, limit, lean, full):
    portions = [(1 << 20) // math.isqrt(grade ** lean) + 1 for grade in range(1, count + 1)]
    largest = limit if full else min(limit, max(-(-total // count), total * portions[0] // sum(portions)))
    least = 1 if total - largest >= count - 1 else 0
    given, rest = [largest] + [least] * (count - 1), total - largest - least * (count - 1)
    while rest > 0:
        free = [i for i in range(1, count) if given[i] < largest] or [i for i in range(1, count) if given[i] < limit]
        whole, left = sum([portions[i] for i in free]), rest
        for i in free:
            addition = min(limit - given[i], max(1, left * portions[i] // whole), rest)
            given[i] = given[i] + addition
            rest = rest - addition
    return np.array(given)


def gaussian(own_key, dims, spread, limit, cuts=(), held_as=jnp.bfloat16):
    values = spread * jax.random.normal(own_key, dims, jnp.float32)
    if cuts:
        values = values * levels(own_key, dims, cuts, -0.22, 0.18)
    return jnp.clip(values, -limit, limit).astype(held_as)


def setup_inputs(seed: int = 0) -> dict:
    streams_of = jax.random.split(jax.random.key(seed), 7)
    front = gaussian(streams_of[0], (RT, N_ROW, CT, N_COL, TILE, TILE), 1.0, 6.0, ((1, 32), (3, 4)), jnp.float32)
    child_tiles = gaussian(streams_of[1], (DEVICES * KT, TILE, TILE), 1.0, 6.0, ((0, 128),), jnp.float32)
    tile_dest_keys = jax.random.split(jax.random.fold_in(streams_of[2], 1), (DEVICES * KT) // KT)
    tile_dest_turns = jax.random.permutation(jax.random.fold_in(streams_of[2], 3), (DEVICES * KT) // KT)
    tile_dest = jax.vmap(lambda own, number: assign_block(jax.random.fold_in(streams_of[2], 2), own, number, KT, DEVICES, 1, 1, 2))(tile_dest_keys, tile_dest_turns).reshape((DEVICES * KT, 1))
    tile_slot = touch_ends(jax.random.randint(streams_of[3], (DEVICES * KT,), 0, RT * CT), jax.random.fold_in(streams_of[3], 1), 0, (RT * CT) - 1).astype(jnp.int32)
    tile_count = draw_tile_count(jax.random.fold_in(streams_of[6], 71), 0)
    diag_inverses = draw_diag_inverses(jax.random.fold_in(streams_of[6], 71), 0)
    return {"front": front, "child_tiles": child_tiles, "tile_dest": tile_dest, "tile_slot": tile_slot, "tile_count": tile_count, "diag_inverses": diag_inverses}


def to_matrix(tiles):
    return tiles.transpose(0, 1, 4, 2, 3, 5).reshape(N, N)


def to_tiles(matrix):
    return matrix.reshape(RT, N_ROW, TILE, CT, N_COL, TILE).transpose(0, 1, 3, 4, 2, 5)


def reference(front, child_tiles, tile_dest, tile_slot, tile_count, diag_inverses):
    high = lax.Precision.HIGHEST
    live = (jnp.arange(KT, dtype=jnp.int32)[None, :] < tile_count[:, None]).reshape(-1)
    dest = tile_dest[:, 0]
    row_dev = dest // N_COL
    col_dev = dest % N_COL
    tile_a = tile_slot // CT
    tile_b = tile_slot % CT
    added = jnp.where(live[:, None, None], child_tiles, jnp.zeros_like(child_tiles))
    assembled = front.at[tile_a, row_dev, tile_b, col_dev].add(added)
    first = to_matrix(assembled)
    index = jnp.arange(N, dtype=jnp.int32)
    panel_one = jnp.dot(first[:, :PANEL], diag_inverses[0], precision=high)
    keep_one = index >= PANEL
    second = first - jnp.where(keep_one[:, None] & keep_one[None, :], jnp.dot(panel_one, panel_one.T, precision=high), jnp.zeros_like(first))
    panel_two = jnp.dot(second[:, PANEL:2 * PANEL], diag_inverses[1], precision=high)
    panel_two = jnp.where(keep_one[:, None], panel_two, jnp.zeros_like(panel_two))
    keep_two = index >= 2 * PANEL
    third = second - jnp.where(keep_two[:, None] & keep_two[None, :], jnp.dot(panel_two, panel_two.T, precision=high), jnp.zeros_like(second))
    factored = third.at[:, :PANEL].set(panel_one).at[:, PANEL:2 * PANEL].set(panel_two)
    return to_tiles(factored)
```

```python
import itertools

import jax
import jax.numpy as jnp
from jax import lax
from jax.experimental import pallas as pl
from jax.experimental.pallas import tpu as pltpu
from jax.sharding import PartitionSpec as P

MESH = pl.DeviceIdType.MESH
F32 = jnp.float32
BF16 = jnp.bfloat16
VMEM_LIMIT = 60 * 2**20
TILE = 128
SHARD = 200


def place(r, c):
    return r // 8, c, (r // 2) % 4, r % 2


def device(x, y, z, k):
    return x * 8 + z * 2 + k, y


def shift(r, c, o):
    x, y, z, k = place(r, c)
    return device((x + o[0]) % 4, (y + o[1]) % 4, (z + o[2]) % 4, (k + o[3]) % 2)


def exchange_order():
    def negated(o):
        return (-o[0]) % 4, (-o[1]) % 4, (-o[2]) % 4, o[3]

    orbits, seen = [], set()
    for o in itertools.product(range(4), range(4), range(4), range(2)):
        if o in seen or o == (0, 0, 0, 0):
            continue
        orbit, a = [], o
        for _ in range(3):
            for b in (a, negated(a)):
                if b not in orbit:
                    orbit.append(b)
            a = (a[1], a[2], a[0], a[3])
        seen |= set(orbit)
        orbits.append(orbit)
    far = sorted(orbits, key=lambda orbit: -sum(min(v, 4 - v) for v in orbit[0][:3]))
    order = []
    while far:
        order += far.pop(0)
        if far:
            order += far.pop(-1)
    return order


ORDER = exchange_order()


def signal(sem, dev):
    pl.semaphore_signal(sem, inc=1, device_id=dev, device_id_type=MESH)


def enter(r, c, line_sem, column_sem):
    barrier = pltpu.get_barrier_semaphore()
    plane = [shift(r, c, (0, 0, dz, dk)) for dz in range(4) for dk in range(2) if dz or dk]
    lines = [shift(r, c, (d, 0, 0, 0)) for d in (1, 2, 3)]
    columns = [shift(r, c, (0, d, 0, 0)) for d in (1, 2, 3)]
    for dev in plane + lines + columns:
        signal(barrier, dev)
    pl.semaphore_wait(barrier, 13)
    for dev in lines:
        signal(line_sem, dev)
    pl.semaphore_wait(line_sem, 3)
    for dev in columns:
        signal(column_sem, dev)
    pl.semaphore_wait(column_sem, 3)


def remote(src, dst, send, recv, dev):
    return pltpu.make_async_remote_copy(
        src_ref=src, dst_ref=dst, send_sem=send, recv_sem=recv, device_id=dev, device_id_type=MESH
    )


def wait_bytes(ref, sem):
    pltpu.make_async_copy(ref, ref, sem).wait()


def exchange_kernel(
    code_ref, code_rows, child_ref, in_ref, codes_ref, packed, line_sem, column_sem, send_sem, recv_sem, code_send, code_recv, own_sem
):
    r = lax.axis_index("row")
    c = lax.axis_index("col")
    me = r * 4 + c
    enter(r, c, line_sem, column_sem)

    for o in ORDER:
        pr, pc = shift(r, c, o)
        remote(
            code_rows.at[pr * 4 + pc], codes_ref.at[me], code_send, code_recv, (pr, pc)
        ).start()
    own_code = pltpu.make_async_copy(code_rows.at[me], codes_ref.at[me], own_sem)
    own_code.start()

    def pack(i, dev_index):
        slot = jnp.maximum(code_ref[dev_index] - 1, 0) % 64
        packed[i] = child_ref[slot]

    for i, o in enumerate(ORDER):
        pr, pc = shift(r, c, o)
        pack(i, pr * 4 + pc)
        remote(packed.at[i], in_ref.at[me], send_sem, recv_sem, (pr, pc)).start()
    last = len(ORDER)
    pack(last, me)
    own_tile = pltpu.make_async_copy(packed.at[last], in_ref.at[me], own_sem)
    own_code.wait()
    own_tile.start()
    own_tile.wait()

    wait_bytes(code_rows.at[pl.ds(0, last)], code_send)
    wait_bytes(codes_ref.at[pl.ds(0, last)], code_recv)
    wait_bytes(packed.at[pl.ds(0, last)], send_sem)
    wait_bytes(in_ref.at[pl.ds(0, last)], recv_sem)


def exchange(code, code_rows, child):
    any_space = pl.BlockSpec(memory_space=pl.ANY)
    vmem = pl.BlockSpec(memory_space=pltpu.VMEM)
    return pl.pallas_call(
        exchange_kernel,
        out_shape=(
            jax.ShapeDtypeStruct((128, TILE, TILE), F32),
            jax.ShapeDtypeStruct((128, 1, 128), jnp.int32),
        ),
        in_specs=[pl.BlockSpec(memory_space=pltpu.SMEM), vmem, vmem],
        out_specs=(any_space, vmem),
        scratch_shapes=[
            pltpu.VMEM((128, TILE, TILE), F32),
            pltpu.SemaphoreType.REGULAR,
            pltpu.SemaphoreType.REGULAR,
        ]
        + [pltpu.SemaphoreType.DMA] * 5,
        compiler_params=pltpu.CompilerParams(
            collective_id=0, has_side_effects=True, vmem_limit_bytes=VMEM_LIMIT
        ),
        name="exchange",
    )(code, code_rows, child)


STEP = 8


def add_kernel(codes_ref, front_ref, in_ref, out_ref, sem, front_sem):
    i = pl.program_id(0)

    @pl.when(i == 0)
    def _():
        copy = pltpu.make_async_copy(front_ref, out_ref, front_sem)
        copy.start()
        copy.wait()

    for s in range(STEP):
        code = codes_ref[i * STEP + s]

        @pl.when(code > 0)
        def _():
            q = (code - 1) // 64
            out_ref[q] += in_ref[s]


def add_tiles(codes, front, incoming):
    return pl.pallas_call(
        add_kernel,
        grid=(128 // STEP,),
        out_shape=jax.ShapeDtypeStruct(front.shape, F32),
        in_specs=[
            pl.BlockSpec(memory_space=pltpu.SMEM),
            pl.BlockSpec(memory_space=pl.ANY),
            pl.BlockSpec((STEP, TILE, TILE), lambda i: (i, 0, 0)),
        ],
        out_specs=pl.BlockSpec(front.shape, lambda i: (0, 0, 0)),
        scratch_shapes=[pltpu.SemaphoreType.DMA, pltpu.SemaphoreType.DMA],
        compiler_params=pltpu.CompilerParams(vmem_limit_bytes=VMEM_LIMIT),
        name="add_tiles",
    )(codes, front, incoming)


def halves(a):
    high = a.astype(BF16)
    return high, (a - high.astype(F32)).astype(BF16)


def dot3(a, b, dims=((1,), (0,))):
    ah, al = a if isinstance(a, tuple) else halves(a)
    bh, bl = b if isinstance(b, tuple) else halves(b)

    def dot(u, v):
        return lax.dot_general(u, v, (dims, ((), ())), preferred_element_type=F32)

    return dot(ah, bh) + (dot(ah, bl) + dot(al, bh))


def panel_kernel(
    field_ref,
    diag_ref,
    all_ref,
    own_ref,
    tiles,
    quarter,
    corner,
    shard,
    line_sem,
    column_sem,
    load_sem,
    local_sem,
    q_send,
    q_recv,
    c_send,
    c_recv,
    o_send,
    o_recv,
    first_recv,
    second_recv,
    twin_recv,
    g_send,
):
    r = lax.axis_index("row")
    c = lax.axis_index("col")
    x, _, z, k = place(r, c)
    load = pltpu.make_async_copy(field_ref.at[:, 0], tiles, load_sem)
    load.start()
    enter(r, c, line_sem, column_sem)
    load.wait()

    target_col = r % 4
    for j in range(4):
        target_row = (r // 4) * 4 + j
        mine = (target_row == r) & (target_col == c)
        src = tiles.at[:, pl.ds(32 * j, 32), :]

        @pl.when(mine)
        def _():
            pltpu.make_async_copy(src, quarter.at[c], q_recv).start()

        @pl.when(jnp.logical_not(mine))
        def _():
            remote(src, quarter.at[c], q_send, q_recv, (target_row, target_col)).start()

    sends_corner = ((r == 2) | (r == 3)) & (c < 2)

    @pl.when(sends_corner)
    def _():
        @pl.loop(0, 64)
        def _(n):
            i = n // 4
            tr = i + 16 * (r - 2)
            tc = n % 4
            src = tiles.at[0, pl.ds(pl.multiple_of(i * 8, 8), 8), :]
            mine = (tr == r) & (tc == c)

            @pl.when(mine)
            def _():
                pltpu.make_async_copy(src, corner.at[c], c_recv).start()

            @pl.when(jnp.logical_not(mine))
            def _():
                remote(src, corner.at[c], c_send, c_recv, (tr, tc)).start()

    wait_bytes(quarter, q_recv)
    wait_bytes(corner, c_recv)

    for d in (1, 3, 2):
        remote(tiles, own_ref.at[c], o_send, o_recv, (r, (c + d) % 4)).start()
    own = pltpu.make_async_copy(tiles, own_ref.at[c], local_sem.at[0])
    own.start()

    left = jnp.concatenate([quarter[0].reshape(96, TILE), quarter[1].reshape(96, TILE)], axis=1)
    extra = jnp.concatenate([corner[0], corner[1]], axis=1)
    shard[0:104, :] = dot3(jnp.concatenate([left, extra], axis=0), diag_ref[0])
    right = jnp.concatenate([quarter[2].reshape(96, TILE), quarter[3].reshape(96, TILE)], axis=1)
    shard[104:200, :] = dot3(right, diag_ref[1])

    def first(d):
        return (((x + (1 - k) * d) % 4) * 8 + ((z + k * d) % 4) * 2 + k, c)

    def second(e):
        return (((x + k * e) % 4) * 8 + ((z + (1 - k) * e) % 4) * 2 + k, c)

    twin = (r + 1 - 2 * k, c)
    for d in (1, 3, 2):
        remote(shard, all_ref.at[r], g_send, first_recv.at[d - 1], first(d)).start()
    for e in (1, 3, 2):
        remote(shard, all_ref.at[r], g_send, second_recv.at[e - 1], second(e)).start()
    remote(shard, all_ref.at[r], g_send, twin_recv, twin).start()
    keep = pltpu.make_async_copy(shard, all_ref.at[r], local_sem.at[1])
    keep.start()
    for d in (1, 3, 2):
        source = first(4 - d)[0]
        block = all_ref.at[source]
        wait_bytes(block, first_recv.at[d - 1])
        for e in (1, 3, 2):
            remote(block, block, g_send, second_recv.at[d * 3 + e - 1], second(e)).start()
        remote(block, block, g_send, twin_recv, twin).start()
    for d in (0, 1, 3, 2):
        for e in (1, 3, 2):
            sx = (x - (1 - k) * d - k * e + 8) % 4
            sz = (z - k * d - (1 - k) * e + 8) % 4
            block = all_ref.at[sx * 8 + sz * 2 + k]
            wait_bytes(block, second_recv.at[d * 3 + e - 1])
            remote(block, block, g_send, twin_recv, twin).start()
    wait_bytes(all_ref.at[pl.ds(0, 16)], twin_recv)
    wait_bytes(all_ref.at[pl.ds(0, 31)], g_send)
    keep.wait()
    own.wait()
    wait_bytes(own_ref.at[pl.ds(0, 3)], o_send)
    wait_bytes(own_ref.at[pl.ds(0, 3)], o_recv)

    row_quarter = tiles.at[:, pl.ds(0, 32), :]
    holds_one = (r % 4) == c
    for j in range(4):

        @pl.when(jnp.logical_not(holds_one & ((r % 4) == j)))
        def _():
            wait_bytes(row_quarter, q_send)

    @pl.when(sends_corner)
    def _():
        @pl.loop(0, 63)
        def _(n):
            wait_bytes(corner.at[0], c_send)

        @pl.when(r == 3)
        def _():
            wait_bytes(corner.at[0], c_send)


def gather_panels(field, diag):
    any_space = pl.BlockSpec(memory_space=pl.ANY)
    vmem = pl.BlockSpec(memory_space=pltpu.VMEM)
    dma = pltpu.SemaphoreType.DMA
    return pl.pallas_call(
        panel_kernel,
        out_shape=(
            jax.ShapeDtypeStruct((32, SHARD, 256), F32),
            jax.ShapeDtypeStruct((4, 3, TILE, TILE), F32),
        ),
        in_specs=[any_space, vmem],
        out_specs=(any_space, any_space),
        scratch_shapes=[
            pltpu.VMEM((3, TILE, TILE), F32),
            pltpu.VMEM((4, 3, 32, TILE), F32),
            pltpu.VMEM((2, 8, TILE), F32),
            pltpu.VMEM((SHARD, 256), F32),
            pltpu.SemaphoreType.REGULAR,
            pltpu.SemaphoreType.REGULAR,
            dma,
            dma((2,)),
            dma,
            dma,
            dma,
            dma,
            dma,
            dma,
            dma((3,)),
            dma((12,)),
            dma,
            dma,
        ],
        compiler_params=pltpu.CompilerParams(
            collective_id=1, has_side_effects=True, vmem_limit_bytes=VMEM_LIMIT
        ),
        name="gather_panels",
    )(field, diag)


def update_kernel(field_ref, all_ref, corner_ref, own_ref, diag_ref, out_ref, row_high, row_low, mix):
    g = pl.program_id(0)
    a = pl.program_id(1)
    r = lax.axis_index("row")
    c = lax.axis_index("col")

    @pl.when((g == 0) & (a == 0))
    def _():
        corner = corner_ref[...].reshape(256, 256)
        one, two = halves(diag_ref[0]), halves(diag_ref[1])
        both = dot3(corner, two, ((0,), (0,)))
        mix[0], mix[1] = halves(both)
        left = jnp.concatenate([own_ref[0].reshape(384, TILE), own_ref[1].reshape(384, TILE)], axis=1)
        right = jnp.concatenate([own_ref[2].reshape(384, TILE), own_ref[3].reshape(384, TILE)], axis=1)
        p_one = dot3(left, one)
        p_two = dot3(right, two) - dot3(p_one, halves(both))
        tile_row = (lax.broadcasted_iota(jnp.int32, (384, 1), 0) // TILE) * 32 + r
        zero = jnp.zeros_like(p_one)
        p_two = jnp.where(tile_row >= 2, p_two, zero)
        panel = jnp.where(
            c < 2,
            jnp.where(c == 0, p_one[:, :TILE], p_one[:, TILE:]),
            jnp.where(c == 2, p_two[:, :TILE], p_two[:, TILE:]),
        )
        out_ref[...] = panel.reshape(3, 1, TILE, TILE)
        rows = jnp.concatenate(
            [jnp.where(tile_row >= 2, p_one, zero), jnp.where(tile_row >= 4, p_two, zero)], axis=1
        )
        row_high[...], row_low[...] = halves(rows)

    @pl.when((g > 0) | (a > 0))
    def _():
        start = pl.multiple_of(a * 32, 32)
        later = pl.multiple_of(a * 32 + 104, 8)
        k_one = all_ref[0, :, pl.ds(start, 32), :].reshape(TILE, 256)
        base = all_ref[0, :, pl.ds(later, 32), :].reshape(TILE, 256)
        k_two = base - dot3(k_one, (mix[0], mix[1]))
        cols = halves(jnp.concatenate([k_one, k_two], axis=1))
        product = dot3((row_high[...], row_low[...]), cols, ((1,), (1,)))
        out_ref[...] = field_ref[...] - product.reshape(3, 1, TILE, TILE)


def update(field, gathered, own, diag):
    whole = lambda shape: pl.BlockSpec(shape, lambda g, a: (0,) * len(shape))
    tiles = pl.BlockSpec((3, 1, TILE, TILE), lambda g, a: (0, a * 8 + g, 0, 0))
    corner = gathered[:, 96:104, :]
    return pl.pallas_call(
        update_kernel,
        grid=(8, 3),
        out_shape=jax.ShapeDtypeStruct(field.shape, F32),
        in_specs=[
            tiles,
            pl.BlockSpec((1, 4, SHARD, 256), lambda g, a: (g, 0, 0, 0)),
            whole((32, 8, 256)),
            whole((4, 3, TILE, TILE)),
            whole((2, 256, 256)),
        ],
        out_specs=tiles,
        scratch_shapes=[
            pltpu.VMEM((384, 512), BF16),
            pltpu.VMEM((384, 512), BF16),
            pltpu.VMEM((2, 256, 256), BF16),
        ],
        compiler_params=pltpu.CompilerParams(vmem_limit_bytes=VMEM_LIMIT),
        name="update",
    )(field, gathered.reshape(8, 4, SHARD, 256), corner, own, diag)


def body(front, child_tiles, tile_dest, tile_slot, tile_count, diag_inverses):
    slot = jnp.arange(64, dtype=jnp.int32)
    hits = (tile_dest[:, 0][None, :] == jnp.arange(128, dtype=jnp.int32)[:, None]) & (slot < tile_count[0])[None, :]
    code = jnp.sum(jnp.where(hits, (tile_slot * 64 + slot + 1)[None, :], 0), axis=1)
    code_rows = jnp.broadcast_to(code[:, None, None], (128, 1, 128))
    incoming, codes = exchange(code, code_rows, child_tiles)
    field = add_tiles(codes[:, 0, 0], front.reshape(72, TILE, TILE), incoming).reshape(3, 24, TILE, TILE)
    gathered, own = gather_panels(field, diag_inverses)
    return update(field, gathered, own, diag_inverses).reshape(front.shape)


def solution(mesh):
    return jax.shard_map(
        body,
        mesh=mesh,
        in_specs=(
            P(None, "row", None, "col", None, None),
            P(("row", "col"), None, None),
            P(("row", "col"), None),
            P(("row", "col")),
            P(("row", "col")),
            P(),
        ),
        out_specs=P(None, "row", None, "col", None, None),
        check_vma=False,
    )
```

```python
import itertools

import jax
import jax.numpy as jnp
from jax import lax
from jax.experimental import pallas as pl
from jax.experimental.pallas import tpu as pltpu
from jax.sharding import PartitionSpec as P

MESH = pl.DeviceIdType.MESH
F32 = jnp.float32
BF16 = jnp.bfloat16
VMEM_LIMIT = 60 * 2**20
TILE = 128
SHARD = 200


def place(r, c):
    return r // 8, c, (r // 2) % 4, r % 2


def device(x, y, z, k):
    return x * 8 + z * 2 + k, y


def shift(r, c, o):
    x, y, z, k = place(r, c)
    return device((x + o[0]) % 4, (y + o[1]) % 4, (z + o[2]) % 4, (k + o[3]) % 2)


def exchange_order():
    def negated(o):
        return (-o[0]) % 4, (-o[1]) % 4, (-o[2]) % 4, o[3]

    orbits, seen = [], set()
    for o in itertools.product(range(4), range(4), range(4), range(2)):
        if o in seen or o == (0, 0, 0, 0):
            continue
        orbit, a = [], o
        for _ in range(3):
            for b in (a, negated(a)):
                if b not in orbit:
                    orbit.append(b)
            a = (a[1], a[2], a[0], a[3])
        seen |= set(orbit)
        orbits.append(orbit)
    far = sorted(orbits, key=lambda orbit: -sum(min(v, 4 - v) for v in orbit[0][:3]))
    order = []
    while far:
        order += far.pop(0)
        if far:
            order += far.pop(-1)
    return order


ORDER = exchange_order()


def signal(sem, dev):
    pl.semaphore_signal(sem, inc=1, device_id=dev, device_id_type=MESH)


def enter(r, c, line_sem, column_sem):
    barrier = pltpu.get_barrier_semaphore()
    plane = [shift(r, c, (0, 0, dz, dk)) for dz in range(4) for dk in range(2) if dz or dk]
    lines = [shift(r, c, (d, 0, 0, 0)) for d in (1, 2, 3)]
    columns = [shift(r, c, (0, d, 0, 0)) for d in (1, 2, 3)]
    for dev in plane + lines + columns:
        signal(barrier, dev)
    pl.semaphore_wait(barrier, 13)
    for dev in lines:
        signal(line_sem, dev)
    pl.semaphore_wait(line_sem, 3)
    for dev in columns:
        signal(column_sem, dev)
    pl.semaphore_wait(column_sem, 3)


def remote(src, dst, send, recv, dev):
    return pltpu.make_async_remote_copy(
        src_ref=src, dst_ref=dst, send_sem=send, recv_sem=recv, device_id=dev, device_id_type=MESH
    )


def wait_bytes(ref, sem):
    pltpu.make_async_copy(ref, ref, sem).wait()


def halves(a):
    high = a.astype(BF16)
    return high, (a - high.astype(F32)).astype(BF16)


def dot3(a, b, dims=((1,), (0,))):
    ah, al = a if isinstance(a, tuple) else halves(a)
    bh, bl = b if isinstance(b, tuple) else halves(b)

    def dot(u, v):
        return lax.dot_general(u, v, (dims, ((), ())), preferred_element_type=F32)

    return dot(ah, bh) + (dot(ah, bl) + dot(al, bh))


def to_rows(column):
    down = lax.broadcasted_iota(jnp.int32, (128, 128), 0)
    across = lax.broadcasted_iota(jnp.int32, (128, 128), 1)
    return jnp.sum(jnp.where(down == across, column, 0), axis=0, keepdims=True)


def assemble_kernel(
    count_ref,
    dest_ref,
    slot_ref,
    child_hbm,
    front_hbm,
    diag_ref,
    field_out,
    all_ref,
    own_ref,
    child,
    field,
    packed,
    incoming,
    code_rows,
    code_in,
    rows,
    sorted_rows,
    picks,
    order,
    tiles,
    quarter,
    corner,
    shard,
    line_sem,
    column_sem,
    child_sem,
    front_sem,
    rows_sem,
    order_sem,
    tile_send,
    tile_recv,
    code_send,
    code_recv,
    keep_sem,
    out_sem,
    local_sem,
    q_send,
    q_recv,
    c_send,
    c_recv,
    o_send,
    o_recv,
    first_recv,
    second_recv,
    twin_recv,
    g_send,
):
    r = lax.axis_index("row")
    c = lax.axis_index("col")
    x, _, z, k = place(r, c)
    me = r * 4 + c
    child_load = pltpu.make_async_copy(child_hbm, child, child_sem)
    child_load.start()
    front_load = pltpu.make_async_copy(front_hbm, field, front_sem)
    front_load.start()

    down = lax.broadcasted_iota(jnp.int32, (128, 64), 0)
    slot = lax.broadcasted_iota(jnp.int32, (128, 64), 1)
    hits = (dest_ref[...] == down) & (slot < count_ref[0])
    code = jnp.sum(jnp.where(hits, slot_ref[...] * 64 + slot + 1, 0), axis=1, keepdims=True)
    code = jnp.broadcast_to(code, (128, 128))
    code_rows[...] = code.reshape(128, 1, 128)
    rows[0:1, :] = jnp.maximum(to_rows(code) - 1, 0) % 64
    to_scalars = pltpu.make_async_copy(rows, picks, rows_sem)
    to_scalars.start()
    enter(r, c, line_sem, column_sem)
    to_scalars.wait()
    child_load.wait()

    for o in ORDER:
        pr, pc = shift(r, c, o)
        remote(
            code_rows.at[pr * 4 + pc], code_in.at[me], code_send, code_recv, (pr, pc)
        ).start()
    code_in[pl.ds(me, 1)] = code_rows[pl.ds(me, 1)]
    for i, o in enumerate(ORDER):
        pr, pc = shift(r, c, o)
        packed[i] = child[picks[0, pr * 4 + pc]]
        remote(packed.at[i], incoming.at[me], tile_send, tile_recv, (pr, pc)).start()
    last = len(ORDER)
    incoming[pl.ds(me, 1)] = child[picks[0, me]].reshape(1, TILE, TILE)

    wait_bytes(code_in.at[pl.ds(0, last)], code_recv)
    wait_bytes(code_rows.at[pl.ds(0, last)], code_send)
    got = code_in[...].reshape(128, 128)
    down = lax.broadcasted_iota(jnp.int32, (128, 128), 0)
    across = lax.broadcasted_iota(jnp.int32, (128, 128), 1)
    place_in = jnp.where(got > 0, (got - 1) // 64, 127)
    key = place_in * 128 + down
    smaller = to_rows(key) < key
    rank = jnp.sum(smaller.astype(jnp.int32), axis=1, keepdims=True)
    at_rank = rank == across
    source = jnp.sum(jnp.where(at_rank, down, 0), axis=0, keepdims=True)
    in_order = jnp.sum(jnp.where(at_rank, place_in, 0), axis=0, keepdims=True)
    before = jnp.sum(jnp.where(rank + 1 == across, place_in, 0), axis=0, keepdims=True)
    starts = (in_order != before) | (lax.broadcasted_iota(jnp.int32, (1, 128), 1) == 0)
    up_to = jnp.sum((place_in <= across).astype(jnp.int32), axis=0, keepdims=True)
    equal = jnp.sum((place_in == across).astype(jnp.int32), axis=0, keepdims=True)
    sorted_rows[0:1, :] = source
    sorted_rows[1:2, :] = starts.astype(jnp.int32)
    sorted_rows[2:3, :] = jnp.maximum(up_to - 1, 0)
    sorted_rows[3:4, :] = equal
    to_scalars = pltpu.make_async_copy(sorted_rows, order, order_sem)
    to_scalars.start()
    to_scalars.wait()
    front_load.wait()
    wait_bytes(packed.at[pl.ds(0, last)], tile_send)
    wait_bytes(incoming.at[pl.ds(0, last)], tile_recv)

    def run(t, total):
        tile = incoming[order[0, t]]
        total = jnp.where(order[1, t] > 0, tile, total + tile)
        packed[t] = total
        return total

    lax.fori_loop(0, 128, run, jnp.zeros((TILE, TILE), F32))

    def assembled(q):
        added = packed[order[2, q]]
        return field[q] + jnp.where(order[3, q] > 0, added, 0.0)

    for a in range(3):
        tiles[a] = assembled(a * 24)

    target_col = r % 4
    for j in range(4):
        target_row = (r // 4) * 4 + j
        mine = (target_row == r) & (target_col == c)
        src = tiles.at[:, pl.ds(32 * j, 32), :]

        @pl.when(mine)
        def _():
            pltpu.make_async_copy(src, quarter.at[c], q_recv).start()

        @pl.when(jnp.logical_not(mine))
        def _():
            remote(src, quarter.at[c], q_send, q_recv, (target_row, target_col)).start()

    sends_corner = ((r == 2) | (r == 3)) & (c < 2)

    @pl.when(sends_corner)
    def _():
        @pl.loop(0, 64)
        def _(n):
            i = n // 4
            tr = i + 16 * (r - 2)
            tc = n % 4
            src = tiles.at[0, pl.ds(pl.multiple_of(i * 8, 8), 8), :]
            mine = (tr == r) & (tc == c)

            @pl.when(mine)
            def _():
                pltpu.make_async_copy(src, corner.at[c], c_recv).start()

            @pl.when(jnp.logical_not(mine))
            def _():
                remote(src, corner.at[c], c_send, c_recv, (tr, tc)).start()

    for a in range(3):

        @pl.loop(1, 24)
        def _(b):
            field[a * 24 + b] = assembled(a * 24 + b)

    field_store = pltpu.make_async_copy(field, field_out, out_sem)
    field_store.start()
    wait_bytes(quarter, q_recv)
    wait_bytes(corner, c_recv)

    for d in (1, 3, 2):
        remote(tiles, own_ref.at[c], o_send, o_recv, (r, (c + d) % 4)).start()
    own = pltpu.make_async_copy(tiles, own_ref.at[c], local_sem.at[0])
    own.start()

    left = jnp.concatenate([quarter[0].reshape(96, TILE), quarter[1].reshape(96, TILE)], axis=1)
    extra = jnp.concatenate([corner[0], corner[1]], axis=1)
    shard[0:104, :] = dot3(jnp.concatenate([left, extra], axis=0), diag_ref[0])
    right = jnp.concatenate([quarter[2].reshape(96, TILE), quarter[3].reshape(96, TILE)], axis=1)
    shard[104:200, :] = dot3(right, diag_ref[1])

    def first(d):
        return (((x + (1 - k) * d) % 4) * 8 + ((z + k * d) % 4) * 2 + k, c)

    def second(e):
        return (((x + k * e) % 4) * 8 + ((z + (1 - k) * e) % 4) * 2 + k, c)

    twin = (r + 1 - 2 * k, c)
    for d in (1, 3, 2):
        remote(shard, all_ref.at[r], g_send, first_recv.at[d - 1], first(d)).start()
    for e in (1, 3, 2):
        remote(shard, all_ref.at[r], g_send, second_recv.at[e - 1], second(e)).start()
    remote(shard, all_ref.at[r], g_send, twin_recv, twin).start()
    keep = pltpu.make_async_copy(shard, all_ref.at[r], local_sem.at[1])
    keep.start()
    for d in (1, 3, 2):
        source = first(4 - d)[0]
        block = all_ref.at[source]
        wait_bytes(block, first_recv.at[d - 1])
        for e in (1, 3, 2):
            remote(block, block, g_send, second_recv.at[d * 3 + e - 1], second(e)).start()
        remote(block, block, g_send, twin_recv, twin).start()
    for d in (0, 1, 3, 2):
        for e in (1, 3, 2):
            sx = (x - (1 - k) * d - k * e + 8) % 4
            sz = (z - k * d - (1 - k) * e + 8) % 4
            block = all_ref.at[sx * 8 + sz * 2 + k]
            wait_bytes(block, second_recv.at[d * 3 + e - 1])
            remote(block, block, g_send, twin_recv, twin).start()
    wait_bytes(all_ref.at[pl.ds(0, 16)], twin_recv)
    wait_bytes(all_ref.at[pl.ds(0, 31)], g_send)
    keep.wait()
    field_store.wait()
    own.wait()
    wait_bytes(own_ref.at[pl.ds(0, 3)], o_send)
    wait_bytes(own_ref.at[pl.ds(0, 3)], o_recv)

    row_quarter = tiles.at[:, pl.ds(0, 32), :]
    holds_one = (r % 4) == c
    for j in range(4):

        @pl.when(jnp.logical_not(holds_one & ((r % 4) == j)))
        def _():
            wait_bytes(row_quarter, q_send)

    @pl.when(sends_corner)
    def _():
        @pl.loop(0, 63)
        def _(n):
            wait_bytes(corner.at[0], c_send)

        @pl.when(r == 3)
        def _():
            wait_bytes(corner.at[0], c_send)


def assemble(count, dest, slot, child, front, diag):
    any_space = pl.BlockSpec(memory_space=pl.ANY)
    vmem = pl.BlockSpec(memory_space=pltpu.VMEM)
    smem = pl.BlockSpec(memory_space=pltpu.SMEM)
    dma = pltpu.SemaphoreType.DMA
    return pl.pallas_call(
        assemble_kernel,
        out_shape=(
            jax.ShapeDtypeStruct((72, TILE, TILE), F32),
            jax.ShapeDtypeStruct((32, SHARD, 256), F32),
            jax.ShapeDtypeStruct((4, 3, TILE, TILE), F32),
        ),
        in_specs=[smem, vmem, vmem, any_space, any_space, vmem],
        out_specs=(any_space,) * 3,
        scratch_shapes=[
            pltpu.VMEM((64, TILE, TILE), F32),
            pltpu.VMEM((72, TILE, TILE), F32),
            pltpu.VMEM((128, TILE, TILE), F32),
            pltpu.VMEM((128, TILE, TILE), F32),
            pltpu.VMEM((128, 1, 128), jnp.int32),
            pltpu.VMEM((128, 1, 128), jnp.int32),
            pltpu.VMEM((8, 128), jnp.int32),
            pltpu.VMEM((8, 128), jnp.int32),
            pltpu.SMEM((8, 128), jnp.int32),
            pltpu.SMEM((8, 128), jnp.int32),
            pltpu.VMEM((3, TILE, TILE), F32),
            pltpu.VMEM((4, 3, 32, TILE), F32),
            pltpu.VMEM((2, 8, TILE), F32),
            pltpu.VMEM((SHARD, 256), F32),
            pltpu.SemaphoreType.REGULAR,
            pltpu.SemaphoreType.REGULAR,
        ]
        + [dma] * 10
        + [dma((2,))]
        + [dma] * 6
        + [dma((3,)), dma((12,)), dma, dma],
        compiler_params=pltpu.CompilerParams(
            collective_id=0, has_side_effects=True, vmem_limit_bytes=VMEM_LIMIT
        ),
        name="assemble",
    )(count, dest, slot, child, front, diag)


def update_kernel(field_ref, all_ref, corner_ref, own_ref, diag_ref, out_ref, row_high, row_low, mix):
    g = pl.program_id(0)
    r = lax.axis_index("row")
    c = lax.axis_index("col")

    @pl.when(g == 0)
    def _():
        corner = corner_ref[...].reshape(256, 256)
        one, two = halves(diag_ref[0]), halves(diag_ref[1])
        both = dot3(corner, two, ((0,), (0,)))
        mix[0], mix[1] = halves(both)
        left = jnp.concatenate([own_ref[0].reshape(384, TILE), own_ref[1].reshape(384, TILE)], axis=1)
        right = jnp.concatenate([own_ref[2].reshape(384, TILE), own_ref[3].reshape(384, TILE)], axis=1)
        p_one = dot3(left, one)
        p_two = dot3(right, two) - dot3(p_one, halves(both))
        tile_row = (lax.broadcasted_iota(jnp.int32, (384, 1), 0) // TILE) * 32 + r
        zero = jnp.zeros_like(p_one)
        p_two = jnp.where(tile_row >= 2, p_two, zero)
        panel = jnp.where(
            c < 2,
            jnp.where(c == 0, p_one[:, :TILE], p_one[:, TILE:]),
            jnp.where(c == 2, p_two[:, :TILE], p_two[:, TILE:]),
        )
        out_ref[:, 0, 0] = panel.reshape(3, TILE, TILE)
        rows = jnp.concatenate(
            [jnp.where(tile_row >= 2, p_one, zero), jnp.where(tile_row >= 4, p_two, zero)], axis=1
        )
        row_high[...], row_low[...] = halves(rows)

    def columns(first):
        n = 3 - first
        k_one = jnp.concatenate(
            [all_ref[0, :, 32 * b : 32 * b + 32, :].reshape(TILE, 256) for b in range(first, 3)]
        )
        base = jnp.concatenate(
            [all_ref[0, :, 32 * b + 104 : 32 * b + 136, :].reshape(TILE, 256) for b in range(first, 3)]
        )
        k_two = base - dot3(k_one, (mix[0], mix[1]))
        cols = halves(jnp.concatenate([k_one, k_two], axis=1))
        product = dot3((row_high[...], row_low[...]), cols, ((1,), (1,)))
        for b in range(n):
            part = product[:, TILE * b : TILE * b + TILE].reshape(3, TILE, TILE)
            out_ref[:, first + b, 0] = field_ref[:, first + b, 0] - part

    @pl.when(g == 0)
    def _():
        columns(1)

    @pl.when(g > 0)
    def _():
        columns(0)


def update(field, gathered, own, diag):
    whole = lambda shape: pl.BlockSpec(shape, lambda g: (0,) * len(shape))
    tiles = pl.BlockSpec((3, 3, 1, TILE, TILE), lambda g: (0, 0, g, 0, 0))
    corner = gathered[:, 96:104, :]
    shape = (3, 3, 8, TILE, TILE)
    return pl.pallas_call(
        update_kernel,
        grid=(8,),
        out_shape=jax.ShapeDtypeStruct(shape, F32),
        in_specs=[
            tiles,
            pl.BlockSpec((1, 4, SHARD, 256), lambda g: (g, 0, 0, 0)),
            whole((32, 8, 256)),
            whole((4, 3, TILE, TILE)),
            whole((2, 256, 256)),
        ],
        out_specs=tiles,
        scratch_shapes=[
            pltpu.VMEM((384, 512), BF16),
            pltpu.VMEM((384, 512), BF16),
            pltpu.VMEM((2, 256, 256), BF16),
        ],
        compiler_params=pltpu.CompilerParams(vmem_limit_bytes=VMEM_LIMIT),
        name="update",
    )(field.reshape(shape), gathered.reshape(8, 4, SHARD, 256), corner, own, diag)


def body(front, child_tiles, tile_dest, tile_slot, tile_count, diag_inverses):
    field, gathered, own = assemble(
        tile_count,
        tile_dest.reshape(1, 64),
        tile_slot.reshape(1, 64),
        child_tiles,
        front.reshape(72, TILE, TILE),
        diag_inverses,
    )
    return update(field, gathered, own, diag_inverses).reshape(front.shape)


def solution(mesh):
    return jax.shard_map(
        body,
        mesh=mesh,
        in_specs=(
            P(None, "row", None, "col", None, None),
            P(("row", "col"), None, None),
            P(("row", "col"), None),
            P(("row", "col")),
            P(("row", "col")),
            P(),
        ),
        out_specs=P(None, "row", None, "col", None, None),
        check_vma=False,
    )
```

```python
import itertools

import jax
import jax.numpy as jnp
from jax import lax
from jax.experimental import pallas as pl
from jax.experimental.pallas import tpu as pltpu
from jax.sharding import PartitionSpec as P

MESH = pl.DeviceIdType.MESH
F32 = jnp.float32
BF16 = jnp.bfloat16
VMEM_LIMIT = 40 * 2**20
TILE = 128
FIRST = 12
EARLY = 96
HALF = ((0, 104), (104, 96))
SHARD = 200


def place(r, c):
    return r // 8, c, (r // 2) % 4, r % 2


def device(x, y, z, k):
    return x * 8 + z * 2 + k, y


def shift(r, c, o):
    x, y, z, k = place(r, c)
    return device((x + o[0]) % 4, (y + o[1]) % 4, (z + o[2]) % 4, (k + o[3]) % 2)


def exchange_order():
    def negated(o):
        return (-o[0]) % 4, (-o[1]) % 4, (-o[2]) % 4, o[3]

    orbits, seen = [], set()
    for o in itertools.product(range(4), range(4), range(4), range(2)):
        if o in seen or o == (0, 0, 0, 0):
            continue
        orbit, a = [], o
        for _ in range(3):
            for b in (a, negated(a)):
                if b not in orbit:
                    orbit.append(b)
            a = (a[1], a[2], a[0], a[3])
        seen |= set(orbit)
        orbits.append(orbit)
    far = sorted(orbits, key=lambda orbit: -sum(min(v, 4 - v) for v in orbit[0][:3]))
    order = []
    while far:
        order += far.pop(0)
        if far:
            order += far.pop(-1)
    return order


ORDER = exchange_order()


def signal(sem, dev):
    pl.semaphore_signal(sem, inc=1, device_id=dev, device_id_type=MESH)


def enter(r, c, line_sem, column_sem):
    barrier = pltpu.get_barrier_semaphore()
    plane = [shift(r, c, (0, 0, dz, dk)) for dz in range(4) for dk in range(2) if dz or dk]
    lines = [shift(r, c, (d, 0, 0, 0)) for d in (1, 2, 3)]
    columns = [shift(r, c, (0, d, 0, 0)) for d in (1, 2, 3)]
    for dev in plane + lines + columns:
        signal(barrier, dev)
    pl.semaphore_wait(barrier, 13)
    for dev in lines:
        signal(line_sem, dev)
    pl.semaphore_wait(line_sem, 3)
    for dev in columns:
        signal(column_sem, dev)
    pl.semaphore_wait(column_sem, 3)


def remote(src, dst, send, recv, dev):
    return pltpu.make_async_remote_copy(
        src_ref=src, dst_ref=dst, send_sem=send, recv_sem=recv, device_id=dev, device_id_type=MESH
    )


def wait_bytes(ref, sem):
    pltpu.make_async_copy(ref, ref, sem).wait()


def halves(a):
    high = a.astype(BF16)
    return high, (a - high.astype(F32)).astype(BF16)


def dot3(a, b, dims=((1,), (0,))):
    ah, al = a if isinstance(a, tuple) else halves(a)
    bh, bl = b if isinstance(b, tuple) else halves(b)

    def dot(u, v):
        return lax.dot_general(u, v, (dims, ((), ())), preferred_element_type=F32)

    if dims == ((1,), (0,)):
        return dot(jnp.concatenate([ah, ah, al], axis=1), jnp.concatenate([bh, bl, bh], axis=0))
    return dot(ah, bh) + (dot(ah, bl) + dot(al, bh))


def to_rows(column):
    down = lax.broadcasted_iota(jnp.int32, (128, 128), 0)
    across = lax.broadcasted_iota(jnp.int32, (128, 128), 1)
    return jnp.sum(jnp.where(down == across, column, 0), axis=0, keepdims=True)


def assemble_kernel(
    count_ref,
    dest_hbm,
    slot_hbm,
    child_hbm,
    front_hbm,
    diag_hbm,
    field,
    all_ref,
    rows_ref,
    diag_ref,
    dest_ref,
    slot_ref,
    child,
    packed,
    incoming,
    incoming_late,
    own_ref,
    code_rows,
    code_in,
    rows,
    sorted_rows,
    picks,
    order,
    tiles,
    quarter,
    corner,
    line_sem,
    column_sem,
    small_sem,
    child_sem,
    front_sem,
    diag_sem,
    rows_sem,
    order_sem,
    tile_send,
    tile_recv,
    late_recv,
    code_send,
    code_recv,
    own_sem,
    q_send,
    q_recv,
    c_send,
    c_recv,
    o_send,
    o_recv,
    first_recv,
    second_recv,
    twin_recv,
    g_send,
):
    r = lax.axis_index("row")
    c = lax.axis_index("col")
    x, _, z, k = place(r, c)
    me = r * 4 + c
    loads = [
        pltpu.make_async_copy(dest_hbm, dest_ref, small_sem.at[0]),
        pltpu.make_async_copy(slot_hbm, slot_ref, small_sem.at[1]),
    ]
    for load in loads:
        load.start()
    child_load = pltpu.make_async_copy(child_hbm, child, child_sem)
    child_load.start()
    front_load = pltpu.make_async_copy(front_hbm, field, front_sem)
    front_load.start()
    diag_load = pltpu.make_async_copy(diag_hbm, diag_ref, diag_sem)
    diag_load.start()
    for load in loads:
        load.wait()

    down = lax.broadcasted_iota(jnp.int32, (128, 64), 0)
    slot = lax.broadcasted_iota(jnp.int32, (128, 64), 1)
    hits = (dest_ref[...] == down) & (slot < count_ref[0])
    code = jnp.sum(jnp.where(hits, slot_ref[...] * 64 + slot + 1, 0), axis=1, keepdims=True)
    code = jnp.broadcast_to(code, (128, 128))
    code_rows[...] = code.reshape(128, 1, 128)
    rows[0:1, :] = jnp.maximum(to_rows(code) - 1, 0) % 64
    to_scalars = pltpu.make_async_copy(rows, picks, rows_sem)
    to_scalars.start()
    enter(r, c, line_sem, column_sem)
    to_scalars.wait()
    child_load.wait()

    def send_codes():
        for i, o in enumerate(ORDER):
            pr, pc = shift(r, c, o)
            remote(code_rows.at[pr * 4 + pc], code_in.at[i], code_send, code_recv, (pr, pc)).start()

    for i, o in enumerate(ORDER):
        if i == FIRST:
            send_codes()
        pr, pc = shift(r, c, o)
        packed[i] = child[picks[0, pr * 4 + pc]]
        landing, recv = (incoming.at[i], tile_recv) if i < EARLY else (incoming_late.at[i - EARLY], late_recv)
        remote(packed.at[i], landing, tile_send, recv, (pr, pc)).start()
    last = len(ORDER)
    code_in[last] = code_rows[me]
    incoming_late[last - EARLY] = child[picks[0, me]]

    wait_bytes(code_in.at[pl.ds(0, last)], code_recv)
    wait_bytes(code_rows.at[pl.ds(0, last)], code_send)
    got = code_in[...].reshape(128, 128)
    down = lax.broadcasted_iota(jnp.int32, (128, 128), 0)
    across = lax.broadcasted_iota(jnp.int32, (128, 128), 1)
    late = (down >= EARLY).astype(jnp.int32)
    place_in = jnp.where(got > 0, (got - 1) // 64, 127)
    group = late * 128 + place_in
    key = group * 128 + down
    smaller = to_rows(key) < key
    rank = jnp.sum(smaller.astype(jnp.int32), axis=1, keepdims=True)
    source = jnp.sum(jnp.where(rank == across, down, 0), axis=0, keepdims=True)
    in_order = jnp.sum(jnp.where(rank == across, group, 0), axis=0, keepdims=True)
    before = jnp.sum(jnp.where(rank + 1 == across, group, 0), axis=0, keepdims=True)
    first = lax.broadcasted_iota(jnp.int32, (1, 128), 1) == 0
    sorted_rows[0:1, :] = source % EARLY
    sorted_rows[1:2, :] = ((in_order != before) | first).astype(jnp.int32)
    for n in range(2):
        up_to = jnp.sum((group <= across + 128 * n).astype(jnp.int32), axis=0, keepdims=True)
        equal = jnp.sum((group == across + 128 * n).astype(jnp.int32), axis=0, keepdims=True)
        sorted_rows[2 + n : 3 + n, :] = jnp.maximum(up_to - 1 - EARLY * n, 0)
        sorted_rows[4 + n : 5 + n, :] = equal
    to_scalars = pltpu.make_async_copy(sorted_rows, order, order_sem)
    to_scalars.start()
    to_scalars.wait()
    front_load.wait()
    diag_load.wait()
    wait_bytes(packed.at[pl.ds(0, last)], tile_send)

    def sums(buffer, start, count):
        def run(t, total):
            tile = buffer[order[0, t]]
            total = jnp.where(order[1, t] > 0, tile, total + tile)
            packed[t] = total
            return total

        lax.fori_loop(start, start + count, run, jnp.zeros((TILE, TILE), F32))

    def assembled(q, n):
        added = packed.at[pl.ds(EARLY * n, (EARLY, 128 - EARLY)[n])][order[2 + n, q]]
        return field[q] + jnp.where(order[4 + n, q] > 0, added, 0.0)

    wait_bytes(incoming, tile_recv)
    sums(incoming, 0, EARLY)

    @pl.loop(0, 72)
    def _(q):
        field[q] = assembled(q, 0)

    wait_bytes(incoming_late.at[pl.ds(0, last - EARLY)], late_recv)
    sums(incoming_late, EARLY, 128 - EARLY)
    for a in range(3):
        tiles[a] = assembled(a * 24, 1)

    target_col = r % 4
    for j in range(4):
        target_row = (r // 4) * 4 + j
        mine = (target_row == r) & (target_col == c)
        src = tiles.at[:, pl.ds(32 * j, 32), :]

        @pl.when(mine)
        def _():
            pltpu.make_async_copy(src, quarter.at[c], q_recv).start()

        @pl.when(jnp.logical_not(mine))
        def _():
            remote(src, quarter.at[c], q_send, q_recv, (target_row, target_col)).start()

    sends_corner = ((r == 2) | (r == 3)) & (c < 2)

    @pl.when(sends_corner)
    def _():
        @pl.loop(0, 64)
        def _(n):
            i = n // 4
            tr = i + 16 * (r - 2)
            tc = n % 4
            src = tiles.at[0, pl.ds(pl.multiple_of(i * 8, 8), 8), :]
            mine = (tr == r) & (tc == c)

            @pl.when(mine)
            def _():
                pltpu.make_async_copy(src, corner.at[c], c_recv).start()

            @pl.when(jnp.logical_not(mine))
            def _():
                remote(src, corner.at[c], c_send, c_recv, (tr, tc)).start()

    for a in range(3):

        @pl.loop(1, 24)
        def _(b):
            field[a * 24 + b] = assembled(a * 24 + b, 1)

    wait_bytes(quarter, q_recv)
    wait_bytes(corner, c_recv)

    for d in (1, 3, 2):
        remote(tiles, own_ref.at[c], o_send, o_recv, (r, (c + d) % 4)).start()
    own = pltpu.make_async_copy(tiles, own_ref.at[c], own_sem)
    own.start()

    left = jnp.concatenate([quarter[0].reshape(96, TILE), quarter[1].reshape(96, TILE)], axis=1)
    extra = jnp.concatenate([corner[0], corner[1]], axis=1)
    right = jnp.concatenate([quarter[2].reshape(96, TILE), quarter[3].reshape(96, TILE)], axis=1)
    one = dot3(jnp.concatenate([left, extra], axis=0), diag_ref[0])
    two = dot3(right, diag_ref[1])
    all_ref[pl.ds(r, 1)] = jnp.concatenate([one, two], axis=0).reshape(1, SHARD, 256)

    def shard_row(da, db):
        sx = (x + (1 - k) * da + k * db + 8) % 4
        sz = (z + k * da + (1 - k) * db + 8) % 4
        return sx * 8 + sz * 2 + k

    def part(da, db, h):
        return all_ref.at[shard_row(da, db), pl.ds(*HALF[h]), :]

    def pass_on(ref, sem, dev):
        remote(ref, ref, g_send, sem, dev).start()

    twin = (r + 1 - 2 * k, c)
    away = (0, -1, 1, 2)

    def to_line(d, h):
        pass_on(part(0, 0, h), first_recv.at[(0 if d == 1 else 2) + h], (shard_row(d, 0), c))

    def to_second(i, h):
        for d in (1, -1) if h == 0 else (-1, 1):
            sem = second_recv.at[i * 6 + (0 if d == 1 else 2) + h]
            pass_on(part(away[i], 0, h), sem, (shard_row(0, d), c))

    def came_first(kind, h):
        i = (1, 2, 3)[kind]
        ref = part(away[i], 0, h)
        wait_bytes(ref, first_recv.at[2 * kind + h])
        if (kind, h) == (0, 0):
            pass_on(ref, first_recv.at[4], (shard_row(1, 0), c))
        if (kind, h) == (1, 1):
            pass_on(ref, first_recv.at[5], (shard_row(-1, 0), c))
        to_second(i, h)
        pass_on(ref, twin_recv, twin)

    def came_second(i, kind, h):
        ref = part(away[i], (-1, 1, 2)[kind], h)
        wait_bytes(ref, second_recv.at[i * 6 + 2 * kind + h])
        if (kind, h) == (0, 0):
            pass_on(ref, second_recv.at[i * 6 + 4], (shard_row(0, 1), c))
        if (kind, h) == (1, 1):
            pass_on(ref, second_recv.at[i * 6 + 5], (shard_row(0, -1), c))
        pass_on(ref, twin_recv, twin)

    for h, d in ((0, 1), (1, -1), (1, 1), (0, -1)):
        to_line(d, h)
    for h in (0, 1):
        to_second(0, h)
    for h in (0, 1):
        pass_on(part(0, 0, h), twin_recv, twin)
    came_first(0, 0)
    came_first(1, 1)
    came_second(0, 0, 0)
    came_second(0, 1, 1)
    came_first(0, 1)
    came_first(1, 0)
    came_second(0, 0, 1)
    came_second(0, 1, 0)
    came_first(2, 0)
    came_first(2, 1)
    came_second(0, 2, 0)
    came_second(0, 2, 1)
    for i in (1, 2, 3):
        came_second(i, 0, 0)
        came_second(i, 1, 1)
        came_second(i, 0, 1)
        came_second(i, 1, 0)

    own.wait()
    wait_bytes(own_ref.at[pl.ds(0, 3)], o_recv)
    left = jnp.concatenate([own_ref[0].reshape(384, TILE), own_ref[1].reshape(384, TILE)], axis=1)
    right = jnp.concatenate([own_ref[2].reshape(384, TILE), own_ref[3].reshape(384, TILE)], axis=1)
    rows_ref[0] = dot3(left, diag_ref[0])
    rows_ref[1] = dot3(right, diag_ref[1])
    for i in (1, 2, 3):
        came_second(i, 2, 0)
        came_second(i, 2, 1)
    wait_bytes(all_ref.at[pl.ds(0, 16)], twin_recv)
    wait_bytes(all_ref.at[pl.ds(0, 31)], g_send)
    wait_bytes(own_ref.at[pl.ds(0, 3)], o_send)

    row_quarter = tiles.at[:, pl.ds(0, 32), :]
    holds_one = (r % 4) == c
    for j in range(4):

        @pl.when(jnp.logical_not(holds_one & ((r % 4) == j)))
        def _():
            wait_bytes(row_quarter, q_send)

    @pl.when(sends_corner)
    def _():
        @pl.loop(0, 63)
        def _(n):
            wait_bytes(corner.at[0], c_send)

        @pl.when(r == 3)
        def _():
            wait_bytes(corner.at[0], c_send)


def assemble(count, dest, slot, child, front, diag):
    any_space = pl.BlockSpec(memory_space=pl.ANY)
    vmem = pl.BlockSpec(memory_space=pltpu.VMEM)
    dma = pltpu.SemaphoreType.DMA
    return pl.pallas_call(
        assemble_kernel,
        out_shape=(
            pltpu.VMEM((72, TILE, TILE), F32),
            pltpu.VMEM((32, SHARD, 256), F32),
            pltpu.VMEM((2, 384, 256), F32),
            pltpu.VMEM((2, 256, 256), F32),
        ),
        in_specs=[pl.BlockSpec(memory_space=pltpu.SMEM)] + [any_space] * 5,
        out_specs=(vmem,) * 4,
        scratch_shapes=[
            pltpu.VMEM((1, 64), jnp.int32),
            pltpu.VMEM((1, 64), jnp.int32),
            pltpu.VMEM((64, TILE, TILE), F32),
            pltpu.VMEM((128, TILE, TILE), F32),
            pltpu.VMEM((EARLY, TILE, TILE), F32),
            pltpu.VMEM((128 - EARLY, TILE, TILE), F32),
            pltpu.VMEM((4, 3, TILE, TILE), F32),
            pltpu.VMEM((128, 1, 128), jnp.int32),
            pltpu.VMEM((128, 1, 128), jnp.int32),
            pltpu.VMEM((8, 128), jnp.int32),
            pltpu.VMEM((8, 128), jnp.int32),
            pltpu.SMEM((8, 128), jnp.int32),
            pltpu.SMEM((8, 128), jnp.int32),
            pltpu.VMEM((3, TILE, TILE), F32),
            pltpu.VMEM((4, 3, 32, TILE), F32),
            pltpu.VMEM((2, 8, TILE), F32),
            pltpu.SemaphoreType.REGULAR,
            pltpu.SemaphoreType.REGULAR,
            dma((2,)),
        ]
        + [dma] * 17
        + [dma((6,)), dma((24,)), dma, dma],
        compiler_params=pltpu.CompilerParams(
            collective_id=0, has_side_effects=True, vmem_limit_bytes=VMEM_LIMIT
        ),
        name="assemble",
    )(count, *[pltpu.with_memory_space_constraint(v, pltpu.HBM) for v in (dest, slot, child, front, diag)])


def update_kernel(field, all_ref, rows_ref, diag_ref, out_hbm, stage, row_parts, panel_ref, out_sem):
    r = lax.axis_index("row")
    c = lax.axis_index("col")
    corner = all_ref[:, 96:104, :].reshape(256, 256)
    both = halves(dot3(corner, diag_ref[1], ((0,), (0,))))
    p_one = rows_ref[0]
    p_two = rows_ref[1] - dot3(p_one, both)
    tile_row = (lax.broadcasted_iota(jnp.int32, (384, 1), 0) // TILE) * 32 + r
    zero = jnp.zeros_like(p_one)
    p_two = jnp.where(tile_row >= 2, p_two, zero)
    panel = jnp.where(
        c < 2,
        jnp.where(c == 0, p_one[:, :TILE], p_one[:, TILE:]),
        jnp.where(c == 2, p_two[:, :TILE], p_two[:, TILE:]),
    )
    panel_ref[...] = panel.reshape(3, TILE, TILE)
    second = jnp.where(tile_row >= 4, p_two, zero)
    first = jnp.where(tile_row >= 2, p_one, zero) - dot3(second, both, ((1,), (1,)))
    high, low = halves(jnp.concatenate([first, second], axis=1))
    row_parts[...] = jnp.concatenate([high, high, low], axis=1)

    @pl.loop(0, 4)
    def _(pair):
        shards = [pl.ds(pl.multiple_of(8 * pair + 4 * n, 4), 4) for n in range(2)]
        both_ways = [
            jnp.concatenate(
                [all_ref[rows, 32 * b + start : 32 * b + start + 32, :].reshape(TILE, 256) for rows in shards for b in range(3)]
            )
            for start in (0, 104)
        ]
        high, low = halves(jnp.concatenate(both_ways, axis=1))
        product = lax.dot_general(
            row_parts[...],
            jnp.concatenate([high, low, high], axis=1),
            (((1,), (1,)), ((), ())),
            preferred_element_type=F32,
        )
        for a in range(3):
            for n in range(2):
                for b in range(3):
                    across = TILE * (3 * n + b)
                    part = product[TILE * a : TILE * a + TILE, across : across + TILE]
                    stage[3 * a + b, 2 * pair + n] = field[3 * a + b, 2 * pair + n] - part

        @pl.when(pair == 0)
        def _():
            for a in range(3):
                stage[3 * a, 0] = panel_ref[a]

        done = pl.ds(2 * pair, 2)
        pltpu.make_async_copy(stage.at[:, done], out_hbm.at[:, done], out_sem).start()

    wait_bytes(stage, out_sem)


def update(field, gathered, rows, diag):
    vmem = pl.BlockSpec(memory_space=pltpu.VMEM)
    shape = (9, 8, TILE, TILE)
    return pl.pallas_call(
        update_kernel,
        out_shape=jax.ShapeDtypeStruct(shape, F32),
        in_specs=[vmem] * 4,
        out_specs=pl.BlockSpec(memory_space=pl.ANY),
        scratch_shapes=[
            pltpu.VMEM(shape, F32),
            pltpu.VMEM((384, 1536), BF16),
            pltpu.VMEM((3, TILE, TILE), F32),
            pltpu.SemaphoreType.DMA,
        ],
        compiler_params=pltpu.CompilerParams(vmem_limit_bytes=VMEM_LIMIT),
        name="update",
    )(field.reshape(shape), gathered, rows, diag)


def body(front, child_tiles, tile_dest, tile_slot, tile_count, diag_inverses):
    field, gathered, rows, diag = assemble(
        tile_count,
        tile_dest.reshape(1, 64),
        tile_slot.reshape(1, 64),
        child_tiles,
        front.reshape(72, TILE, TILE),
        diag_inverses,
    )
    return update(field, gathered, rows, diag).reshape(front.shape)


def solution(mesh):
    return jax.shard_map(
        body,
        mesh=mesh,
        in_specs=(
            P(None, "row", None, "col", None, None),
            P(("row", "col"), None, None),
            P(("row", "col"), None),
            P(("row", "col")),
            P(("row", "col")),
            P(),
        ),
        out_specs=P(None, "row", None, "col", None, None),
        check_vma=False,
    )
```

```python
import itertools

import jax
import jax.numpy as jnp
from jax import lax
from jax.experimental import pallas as pl
from jax.experimental.pallas import tpu as pltpu
from jax.sharding import PartitionSpec as P

MESH = pl.DeviceIdType.MESH
F32 = jnp.float32
BF16 = jnp.bfloat16
VMEM_LIMIT = 40 * 2**20
TILE = 128
FIRST = 12
EARLY = 96
PIECES = ((0, 56), (56, 48), (104, 48), (152, 48))
SHARD = 200


def place(r, c):
    return r // 8, c, (r // 2) % 4, r % 2


def device(x, y, z, k):
    return x * 8 + z * 2 + k, y


def shift(r, c, o):
    x, y, z, k = place(r, c)
    return device((x + o[0]) % 4, (y + o[1]) % 4, (z + o[2]) % 4, (k + o[3]) % 2)


def exchange_order():
    def negated(o):
        return (-o[0]) % 4, (-o[1]) % 4, (-o[2]) % 4, o[3]

    orbits, seen = [], set()
    for o in itertools.product(range(4), range(4), range(4), range(2)):
        if o in seen or o == (0, 0, 0, 0):
            continue
        orbit, a = [], o
        for _ in range(3):
            for b in (a, negated(a)):
                if b not in orbit:
                    orbit.append(b)
            a = (a[1], a[2], a[0], a[3])
        seen |= set(orbit)
        orbits.append(orbit)
    far = sorted(orbits, key=lambda orbit: -sum(min(v, 4 - v) for v in orbit[0][:3]))
    order = []
    while far:
        order += far.pop(0)
        if far:
            order += far.pop(-1)
    return order


ORDER = exchange_order()


def signal(sem, dev):
    pl.semaphore_signal(sem, inc=1, device_id=dev, device_id_type=MESH)


def enter(r, c, line_sem, column_sem):
    barrier = pltpu.get_barrier_semaphore()
    plane = [shift(r, c, (0, 0, dz, dk)) for dz in range(4) for dk in range(2) if dz or dk]
    lines = [shift(r, c, (d, 0, 0, 0)) for d in (1, 2, 3)]
    columns = [shift(r, c, (0, d, 0, 0)) for d in (1, 2, 3)]
    for dev in plane + lines + columns:
        signal(barrier, dev)
    pl.semaphore_wait(barrier, 13)
    for dev in lines:
        signal(line_sem, dev)
    pl.semaphore_wait(line_sem, 3)
    for dev in columns:
        signal(column_sem, dev)
    pl.semaphore_wait(column_sem, 3)


def remote(src, dst, send, recv, dev):
    return pltpu.make_async_remote_copy(
        src_ref=src, dst_ref=dst, send_sem=send, recv_sem=recv, device_id=dev, device_id_type=MESH
    )


def wait_bytes(ref, sem):
    pltpu.make_async_copy(ref, ref, sem).wait()


def halves(a):
    high = a.astype(BF16)
    return high, (a - high.astype(F32)).astype(BF16)


def dot3(a, b, dims=((1,), (0,))):
    ah, al = a if isinstance(a, tuple) else halves(a)
    bh, bl = b if isinstance(b, tuple) else halves(b)

    def dot(u, v):
        return lax.dot_general(u, v, (dims, ((), ())), preferred_element_type=F32)

    if dims == ((1,), (0,)):
        return dot(jnp.concatenate([ah, ah, al], axis=1), jnp.concatenate([bh, bl, bh], axis=0))
    return dot(ah, bh) + (dot(ah, bl) + dot(al, bh))


def to_rows(column):
    down = lax.broadcasted_iota(jnp.int32, (128, 128), 0)
    across = lax.broadcasted_iota(jnp.int32, (128, 128), 1)
    return jnp.sum(jnp.where(down == across, column, 0), axis=0, keepdims=True)


def assemble_kernel(
    count_ref,
    dest_hbm,
    slot_hbm,
    child_hbm,
    front_hbm,
    diag_hbm,
    field,
    all_ref,
    rows_ref,
    diag_ref,
    dest_ref,
    slot_ref,
    child,
    packed,
    summed,
    incoming,
    incoming_late,
    own_ref,
    diag_parts,
    code_rows,
    code_in,
    rows,
    sorted_rows,
    picks,
    order,
    tiles,
    quarter,
    corner,
    line_sem,
    column_sem,
    small_sem,
    child_sem,
    front_sem,
    diag_sem,
    rows_sem,
    order_sem,
    tile_send,
    tile_recv,
    late_recv,
    code_send,
    code_recv,
    own_sem,
    q_send,
    q_recv,
    c_send,
    c_recv,
    o_send,
    o_recv,
    first_recv,
    second_recv,
    twin_recv,
    g_send,
):
    r = lax.axis_index("row")
    c = lax.axis_index("col")
    x, _, z, k = place(r, c)
    me = r * 4 + c
    loads = [
        pltpu.make_async_copy(dest_hbm, dest_ref, small_sem.at[0]),
        pltpu.make_async_copy(slot_hbm, slot_ref, small_sem.at[1]),
    ]
    for load in loads:
        load.start()
    child_load = pltpu.make_async_copy(child_hbm, child, child_sem)
    child_load.start()
    front_load = pltpu.make_async_copy(front_hbm, field, front_sem)
    front_load.start()
    diag_load = pltpu.make_async_copy(diag_hbm, diag_ref, diag_sem)
    diag_load.start()
    for load in loads:
        load.wait()

    down = lax.broadcasted_iota(jnp.int32, (128, 64), 0)
    slot = lax.broadcasted_iota(jnp.int32, (128, 64), 1)
    hits = (dest_ref[...] == down) & (slot < count_ref[0])
    code = jnp.sum(jnp.where(hits, slot_ref[...] * 64 + slot + 1, 0), axis=1, keepdims=True)
    code = jnp.broadcast_to(code, (128, 128))
    code_rows[...] = code.reshape(128, 1, 128)
    rows[0:1, :] = jnp.maximum(to_rows(code) - 1, 0) % 64
    to_scalars = pltpu.make_async_copy(rows, picks, rows_sem)
    to_scalars.start()
    enter(r, c, line_sem, column_sem)
    to_scalars.wait()
    child_load.wait()

    def send_codes():
        for i, o in enumerate(ORDER):
            pr, pc = shift(r, c, o)
            remote(code_rows.at[pr * 4 + pc], code_in.at[i], code_send, code_recv, (pr, pc)).start()

    for i, o in enumerate(ORDER):
        if i == FIRST:
            send_codes()
        pr, pc = shift(r, c, o)
        packed[i] = child[picks[0, pr * 4 + pc]]
        landing, recv = (incoming.at[i], tile_recv) if i < EARLY else (incoming_late.at[i - EARLY], late_recv)
        remote(packed.at[i], landing, tile_send, recv, (pr, pc)).start()
    last = len(ORDER)
    code_in[last] = code_rows[me]
    incoming_late[last - EARLY] = child[picks[0, me]]

    wait_bytes(code_in.at[pl.ds(0, last)], code_recv)
    wait_bytes(code_rows.at[pl.ds(0, last)], code_send)
    got = code_in[...].reshape(128, 128)
    down = lax.broadcasted_iota(jnp.int32, (128, 128), 0)
    across = lax.broadcasted_iota(jnp.int32, (128, 128), 1)
    late = (down >= EARLY).astype(jnp.int32)
    place_in = jnp.where(got > 0, (got - 1) // 64, 127)
    group = late * 128 + place_in
    key = group * 128 + down
    smaller = to_rows(key) < key
    rank = jnp.sum(smaller.astype(jnp.int32), axis=1, keepdims=True)
    source = jnp.sum(jnp.where(rank == across, down, 0), axis=0, keepdims=True)
    in_order = jnp.sum(jnp.where(rank == across, group, 0), axis=0, keepdims=True)
    before = jnp.sum(jnp.where(rank + 1 == across, group, 0), axis=0, keepdims=True)
    first = lax.broadcasted_iota(jnp.int32, (1, 128), 1) == 0
    sorted_rows[0:1, :] = source % EARLY
    sorted_rows[1:2, :] = ((in_order != before) | first).astype(jnp.int32)
    for n in range(2):
        up_to = jnp.sum((group <= across + 128 * n).astype(jnp.int32), axis=0, keepdims=True)
        equal = jnp.sum((group == across + 128 * n).astype(jnp.int32), axis=0, keepdims=True)
        sorted_rows[2 + n : 3 + n, :] = jnp.maximum(up_to - 1 - EARLY * n, 0)
        sorted_rows[4 + n : 5 + n, :] = equal
    to_scalars = pltpu.make_async_copy(sorted_rows, order, order_sem)
    to_scalars.start()
    to_scalars.wait()
    front_load.wait()
    diag_load.wait()
    for n in range(2):
        high, low = halves(diag_ref[n])
        diag_parts[n] = jnp.concatenate([high, low, high], axis=0)

    def by_diag(a, n):
        high, low = halves(a)
        return lax.dot_general(
            jnp.concatenate([high, high, low], axis=1),
            diag_parts[n],
            (((1,), (0,)), ((), ())),
            preferred_element_type=F32,
        )

    def sums(buffer, start, count):
        def run(t, total):
            tile = buffer[order[0, t]]
            total = jnp.where(order[1, t] > 0, tile, total + tile)
            summed[t] = total
            return total

        lax.fori_loop(start, start + count, run, jnp.zeros((TILE, TILE), F32))

    def assembled(q, n):
        added = summed.at[pl.ds(EARLY * n, (EARLY, 128 - EARLY)[n])][order[2 + n, q]]
        return field[q] + jnp.where(order[4 + n, q] > 0, added, 0.0)

    wait_bytes(incoming, tile_recv)
    sums(incoming, 0, EARLY)

    @pl.loop(0, 72)
    def _(q):
        field[q] = assembled(q, 0)

    wait_bytes(incoming_late.at[pl.ds(0, last - EARLY)], late_recv)
    sums(incoming_late, EARLY, 128 - EARLY)
    for a in range(3):
        tiles[a] = assembled(a * 24, 1)

    target_col = r % 4
    for j in range(4):
        target_row = (r // 4) * 4 + j
        mine = (target_row == r) & (target_col == c)
        src = tiles.at[:, pl.ds(32 * j, 32), :]

        @pl.when(mine)
        def _():
            pltpu.make_async_copy(src, quarter.at[c], q_recv).start()

        @pl.when(jnp.logical_not(mine))
        def _():
            remote(src, quarter.at[c], q_send, q_recv, (target_row, target_col)).start()

    sends_corner = ((r == 2) | (r == 3)) & (c < 2)

    @pl.when(sends_corner)
    def _():
        @pl.loop(0, 64)
        def _(n):
            i = n // 4
            tr = i + 16 * (r - 2)
            tc = n % 4
            src = tiles.at[0, pl.ds(pl.multiple_of(i * 8, 8), 8), :]
            mine = (tr == r) & (tc == c)

            @pl.when(mine)
            def _():
                pltpu.make_async_copy(src, corner.at[c], c_recv).start()

            @pl.when(jnp.logical_not(mine))
            def _():
                remote(src, corner.at[c], c_send, c_recv, (tr, tc)).start()

    for a in range(3):

        @pl.loop(1, 24)
        def _(b):
            field[a * 24 + b] = assembled(a * 24 + b, 1)

    wait_bytes(quarter, q_recv)
    wait_bytes(corner, c_recv)

    for d in (1, 3, 2):
        remote(tiles, own_ref.at[c], o_send, o_recv, (r, (c + d) % 4)).start()
    own = pltpu.make_async_copy(tiles, own_ref.at[c], own_sem)
    own.start()

    left = jnp.concatenate([quarter[0].reshape(96, TILE), quarter[1].reshape(96, TILE)], axis=1)
    extra = jnp.concatenate([corner[0], corner[1]], axis=1)
    right = jnp.concatenate([quarter[2].reshape(96, TILE), quarter[3].reshape(96, TILE)], axis=1)
    one = by_diag(jnp.concatenate([left, extra], axis=0), 0)
    two = by_diag(right, 1)
    all_ref[pl.ds(r, 1)] = jnp.concatenate([one, two], axis=0).reshape(1, SHARD, 256)

    def shard_row(da, db):
        sx = (x + (1 - k) * da + k * db + 8) % 4
        sz = (z + k * da + (1 - k) * db + 8) % 4
        return sx * 8 + sz * 2 + k

    def piece(da, db, p):
        return all_ref.at[shard_row(da, db), pl.ds(*PIECES[p]), :]

    def pass_on(ref, sem, dev):
        remote(ref, ref, g_send, sem, dev).start()

    twin = (r + 1 - 2 * k, c)
    away = (0, -1, 1, 2)
    count = len(PIECES)
    up = range(count // 2)
    down = range(count // 2, count)

    def to_second(i, p):
        for d in (1, -1) if p in up else (-1, 1):
            sem = second_recv.at[(3 * i + (0 if d == 1 else 1)) * count + p]
            pass_on(piece(away[i], 0, p), sem, (shard_row(0, d), c))

    def came_first(way, p):
        ref = piece(away[way + 1], 0, p)
        wait_bytes(ref, first_recv.at[way * count + p])
        if way == 0 and p in up:
            pass_on(ref, first_recv.at[2 * count + p], (shard_row(1, 0), c))
        if way == 1 and p in down:
            pass_on(ref, first_recv.at[2 * count + p], (shard_row(-1, 0), c))
        to_second(way + 1, p)
        pass_on(ref, twin_recv, twin)

    def came_second(i, way, p):
        ref = piece(away[i], (-1, 1, 2)[way], p)
        wait_bytes(ref, second_recv.at[(3 * i + way) * count + p])
        if way == 0 and p in up:
            pass_on(ref, second_recv.at[(3 * i + 2) * count + p], (shard_row(0, 1), c))
        if way == 1 and p in down:
            pass_on(ref, second_recv.at[(3 * i + 2) * count + p], (shard_row(0, -1), c))
        pass_on(ref, twin_recv, twin)

    passed = [(way, pair[way]) for pair in zip(up, down) for way in (0, 1)]
    kept = [(way, pair[1 - way]) for pair in zip(up, down) for way in (0, 1)]
    for way, p in passed + kept:
        d = 1 - 2 * way
        pass_on(piece(0, 0, p), first_recv.at[way * count + p], (shard_row(d, 0), c))
    for p in range(count):
        to_second(0, p)
    for p in range(count):
        pass_on(piece(0, 0, p), twin_recv, twin)
    for some in (passed, kept):
        for way, p in some:
            came_first(way, p)
        for way, p in some:
            came_second(0, way, p)
    for p in range(count):
        came_first(2, p)
    for p in range(count):
        came_second(0, 2, p)
    for i in (1, 2, 3):
        for way, p in passed + kept:
            came_second(i, way, p)

    for i in (1, 2, 3):
        for p in range(count):
            came_second(i, 2, p)
    own.wait()
    wait_bytes(own_ref.at[pl.ds(0, 3)], o_recv)
    left = jnp.concatenate([own_ref[0].reshape(384, TILE), own_ref[1].reshape(384, TILE)], axis=1)
    right = jnp.concatenate([own_ref[2].reshape(384, TILE), own_ref[3].reshape(384, TILE)], axis=1)
    rows_ref[0] = by_diag(left, 0)
    rows_ref[1] = by_diag(right, 1)
    wait_bytes(all_ref.at[pl.ds(0, 16)], twin_recv)
    wait_bytes(all_ref.at[pl.ds(0, 31)], g_send)
    wait_bytes(own_ref.at[pl.ds(0, 3)], o_send)

    wait_bytes(packed.at[pl.ds(0, last)], tile_send)
    row_quarter = tiles.at[:, pl.ds(0, 32), :]
    holds_one = (r % 4) == c
    for j in range(4):

        @pl.when(jnp.logical_not(holds_one & ((r % 4) == j)))
        def _():
            wait_bytes(row_quarter, q_send)

    @pl.when(sends_corner)
    def _():
        @pl.loop(0, 63)
        def _(n):
            wait_bytes(corner.at[0], c_send)

        @pl.when(r == 3)
        def _():
            wait_bytes(corner.at[0], c_send)


def assemble(count, dest, slot, child, front, diag):
    any_space = pl.BlockSpec(memory_space=pl.ANY)
    vmem = pl.BlockSpec(memory_space=pltpu.VMEM)
    dma = pltpu.SemaphoreType.DMA
    return pl.pallas_call(
        assemble_kernel,
        out_shape=(
            pltpu.VMEM((72, TILE, TILE), F32),
            pltpu.VMEM((32, SHARD, 256), F32),
            pltpu.VMEM((2, 384, 256), F32),
            pltpu.VMEM((2, 256, 256), F32),
        ),
        in_specs=[pl.BlockSpec(memory_space=pltpu.SMEM)] + [any_space] * 5,
        out_specs=(vmem,) * 4,
        scratch_shapes=[
            pltpu.VMEM((1, 64), jnp.int32),
            pltpu.VMEM((1, 64), jnp.int32),
            pltpu.VMEM((64, TILE, TILE), F32),
            pltpu.VMEM((128, TILE, TILE), F32),
            pltpu.VMEM((128, TILE, TILE), F32),
            pltpu.VMEM((EARLY, TILE, TILE), F32),
            pltpu.VMEM((128 - EARLY, TILE, TILE), F32),
            pltpu.VMEM((4, 3, TILE, TILE), F32),
            pltpu.VMEM((2, 768, 256), BF16),
            pltpu.VMEM((128, 1, 128), jnp.int32),
            pltpu.VMEM((128, 1, 128), jnp.int32),
            pltpu.VMEM((8, 128), jnp.int32),
            pltpu.VMEM((8, 128), jnp.int32),
            pltpu.SMEM((8, 128), jnp.int32),
            pltpu.SMEM((8, 128), jnp.int32),
            pltpu.VMEM((3, TILE, TILE), F32),
            pltpu.VMEM((4, 3, 32, TILE), F32),
            pltpu.VMEM((2, 8, TILE), F32),
            pltpu.SemaphoreType.REGULAR,
            pltpu.SemaphoreType.REGULAR,
            dma((2,)),
        ]
        + [dma] * 17
        + [dma((12,)), dma((48,)), dma, dma],
        compiler_params=pltpu.CompilerParams(
            collective_id=0, has_side_effects=True, vmem_limit_bytes=VMEM_LIMIT
        ),
        name="assemble",
    )(count, *[pltpu.with_memory_space_constraint(v, pltpu.HBM) for v in (dest, slot, child, front, diag)])


def update_kernel(field, all_ref, rows_ref, diag_ref, out_hbm, stage, row_parts, panel_ref, out_sem):
    r = lax.axis_index("row")
    c = lax.axis_index("col")
    corner = all_ref[:, 96:104, :].reshape(256, 256)
    both = halves(dot3(corner, diag_ref[1], ((0,), (0,))))
    p_one = rows_ref[0]
    p_two = rows_ref[1] - dot3(p_one, both)
    tile_row = (lax.broadcasted_iota(jnp.int32, (384, 1), 0) // TILE) * 32 + r
    zero = jnp.zeros_like(p_one)
    p_two = jnp.where(tile_row >= 2, p_two, zero)
    panel = jnp.where(
        c < 2,
        jnp.where(c == 0, p_one[:, :TILE], p_one[:, TILE:]),
        jnp.where(c == 2, p_two[:, :TILE], p_two[:, TILE:]),
    )
    panel_ref[...] = panel.reshape(3, TILE, TILE)
    second = jnp.where(tile_row >= 4, p_two, zero)
    first = jnp.where(tile_row >= 2, p_one, zero) - dot3(second, both, ((1,), (1,)))
    high, low = halves(jnp.concatenate([first, second], axis=1))
    row_parts[...] = jnp.concatenate([high, high, low], axis=1)

    @pl.loop(0, 4)
    def _(pair):
        shards = [pl.ds(pl.multiple_of(8 * pair + 4 * n, 4), 4) for n in range(2)]
        both_ways = [
            jnp.concatenate(
                [all_ref[rows, 32 * b + start : 32 * b + start + 32, :].reshape(TILE, 256) for rows in shards for b in range(3)]
            )
            for start in (0, 104)
        ]
        high, low = halves(jnp.concatenate(both_ways, axis=1))
        product = lax.dot_general(
            row_parts[...],
            jnp.concatenate([high, low, high], axis=1),
            (((1,), (1,)), ((), ())),
            preferred_element_type=F32,
        )
        for a in range(3):
            for n in range(2):
                for b in range(3):
                    across = TILE * (3 * n + b)
                    part = product[TILE * a : TILE * a + TILE, across : across + TILE]
                    stage[3 * a + b, 2 * pair + n] = field[3 * a + b, 2 * pair + n] - part

        @pl.when(pair == 0)
        def _():
            for a in range(3):
                stage[3 * a, 0] = panel_ref[a]

        done = pl.ds(2 * pair, 2)
        pltpu.make_async_copy(stage.at[:, done], out_hbm.at[:, done], out_sem).start()

    wait_bytes(stage, out_sem)


def update(field, gathered, rows, diag):
    vmem = pl.BlockSpec(memory_space=pltpu.VMEM)
    shape = (9, 8, TILE, TILE)
    return pl.pallas_call(
        update_kernel,
        out_shape=jax.ShapeDtypeStruct(shape, F32),
        in_specs=[vmem] * 4,
        out_specs=pl.BlockSpec(memory_space=pl.ANY),
        scratch_shapes=[
            pltpu.VMEM(shape, F32),
            pltpu.VMEM((384, 1536), BF16),
            pltpu.VMEM((3, TILE, TILE), F32),
            pltpu.SemaphoreType.DMA,
        ],
        compiler_params=pltpu.CompilerParams(vmem_limit_bytes=VMEM_LIMIT),
        name="update",
    )(field.reshape(shape), gathered, rows, diag)


def body(front, child_tiles, tile_dest, tile_slot, tile_count, diag_inverses):
    field, gathered, rows, diag = assemble(
        tile_count,
        tile_dest.reshape(1, 64),
        tile_slot.reshape(1, 64),
        child_tiles,
        front.reshape(72, TILE, TILE),
        diag_inverses,
    )
    return update(field, gathered, rows, diag).reshape(front.shape)


def solution(mesh):
    return jax.shard_map(
        body,
        mesh=mesh,
        in_specs=(
            P(None, "row", None, "col", None, None),
            P(("row", "col"), None, None),
            P(("row", "col"), None),
            P(("row", "col")),
            P(("row", "col")),
            P(),
        ),
        out_specs=P(None, "row", None, "col", None, None),
        check_vma=False,
    )
```

```python
import itertools

import jax
import jax.numpy as jnp
from jax import lax
from jax.experimental import pallas as pl
from jax.experimental.pallas import tpu as pltpu
from jax.sharding import PartitionSpec as P

MESH = pl.DeviceIdType.MESH
F32 = jnp.float32
BF16 = jnp.bfloat16
VMEM_LIMIT = 40 * 2**20
TILE = 128
FIRST = 12
EARLY = 96
PIECES = ((0, 56), (56, 48), (104, 48), (152, 48))
SHARD = 200


def place(r, c):
    return r // 8, c, (r // 2) % 4, r % 2


def device(x, y, z, k):
    return x * 8 + z * 2 + k, y


def shift(r, c, o):
    x, y, z, k = place(r, c)
    return device((x + o[0]) % 4, (y + o[1]) % 4, (z + o[2]) % 4, (k + o[3]) % 2)


def exchange_order():
    def negated(o):
        return (-o[0]) % 4, (-o[1]) % 4, (-o[2]) % 4, o[3]

    orbits, seen = [], set()
    for o in itertools.product(range(4), range(4), range(4), range(2)):
        if o in seen or o == (0, 0, 0, 0):
            continue
        orbit, a = [], o
        for _ in range(3):
            for b in (a, negated(a)):
                if b not in orbit:
                    orbit.append(b)
            a = (a[1], a[2], a[0], a[3])
        seen |= set(orbit)
        orbits.append(orbit)
    far = sorted(orbits, key=lambda orbit: -sum(min(v, 4 - v) for v in orbit[0][:3]))
    order = []
    while far:
        order += far.pop(0)
        if far:
            order += far.pop(-1)
    return order


ORDER = exchange_order()


def signal(sem, dev):
    pl.semaphore_signal(sem, inc=1, device_id=dev, device_id_type=MESH)


def enter(r, c, line_sem, column_sem):
    barrier = pltpu.get_barrier_semaphore()
    plane = [shift(r, c, (0, 0, dz, dk)) for dz in range(4) for dk in range(2) if dz or dk]
    lines = [shift(r, c, (d, 0, 0, 0)) for d in (1, 2, 3)]
    columns = [shift(r, c, (0, d, 0, 0)) for d in (1, 2, 3)]
    for dev in plane + lines + columns:
        signal(barrier, dev)
    pl.semaphore_wait(barrier, 13)
    for dev in lines:
        signal(line_sem, dev)
    pl.semaphore_wait(line_sem, 3)
    for dev in columns:
        signal(column_sem, dev)
    pl.semaphore_wait(column_sem, 3)


def remote(src, dst, send, recv, dev):
    return pltpu.make_async_remote_copy(
        src_ref=src, dst_ref=dst, send_sem=send, recv_sem=recv, device_id=dev, device_id_type=MESH
    )


def wait_bytes(ref, sem):
    pltpu.make_async_copy(ref, ref, sem).wait()


def halves(a):
    high = a.astype(BF16)
    return high, (a - high.astype(F32)).astype(BF16)


def dot3(a, b, dims=((1,), (0,))):
    ah, al = a if isinstance(a, tuple) else halves(a)
    bh, bl = b if isinstance(b, tuple) else halves(b)

    def dot(u, v):
        return lax.dot_general(u, v, (dims, ((), ())), preferred_element_type=F32)

    if dims == ((1,), (0,)):
        return dot(jnp.concatenate([ah, ah, al], axis=1), jnp.concatenate([bh, bl, bh], axis=0))
    return dot(ah, bh) + (dot(ah, bl) + dot(al, bh))


def to_rows(column):
    down = lax.broadcasted_iota(jnp.int32, (128, 128), 0)
    across = lax.broadcasted_iota(jnp.int32, (128, 128), 1)
    return jnp.sum(jnp.where(down == across, column, 0), axis=0, keepdims=True)


def assemble_kernel(
    count_ref,
    dest_hbm,
    slot_hbm,
    child_hbm,
    front_hbm,
    diag_hbm,
    field,
    all_ref,
    rows_ref,
    diag_ref,
    dest_ref,
    slot_ref,
    child,
    packed,
    summed,
    incoming,
    incoming_late,
    own_ref,
    diag_parts,
    code_rows,
    code_in,
    rows,
    sorted_rows,
    picks,
    order,
    tiles,
    quarter,
    corner,
    line_sem,
    column_sem,
    small_sem,
    child_sem,
    front_sem,
    diag_sem,
    rows_sem,
    order_sem,
    tile_send,
    tile_recv,
    late_recv,
    code_send,
    code_recv,
    own_sem,
    q_send,
    q_recv,
    c_send,
    c_recv,
    o_send,
    o_recv,
    first_recv,
    second_recv,
    twin_recv,
    g_send,
):
    r = lax.axis_index("row")
    c = lax.axis_index("col")
    x, _, z, k = place(r, c)
    me = r * 4 + c
    loads = [
        pltpu.make_async_copy(dest_hbm, dest_ref, small_sem.at[0]),
        pltpu.make_async_copy(slot_hbm, slot_ref, small_sem.at[1]),
    ]
    for load in loads:
        load.start()
    child_load = pltpu.make_async_copy(child_hbm, child, child_sem)
    child_load.start()
    front_load = pltpu.make_async_copy(front_hbm, field, front_sem)
    front_load.start()
    diag_load = pltpu.make_async_copy(diag_hbm, diag_ref, diag_sem)
    diag_load.start()
    for load in loads:
        load.wait()

    down = lax.broadcasted_iota(jnp.int32, (128, 64), 0)
    slot = lax.broadcasted_iota(jnp.int32, (128, 64), 1)
    hits = (dest_ref[...] == down) & (slot < count_ref[0])
    code = jnp.sum(jnp.where(hits, slot_ref[...] * 64 + slot + 1, 0), axis=1, keepdims=True)
    code = jnp.broadcast_to(code, (128, 128))
    code_rows[...] = code.reshape(128, 1, 128)
    rows[0:1, :] = jnp.maximum(to_rows(code) - 1, 0) % 64
    to_scalars = pltpu.make_async_copy(rows, picks, rows_sem)
    to_scalars.start()
    enter(r, c, line_sem, column_sem)
    to_scalars.wait()
    child_load.wait()

    def send_codes():
        for i, o in enumerate(ORDER):
            pr, pc = shift(r, c, o)
            remote(code_rows.at[pr * 4 + pc], code_in.at[i], code_send, code_recv, (pr, pc)).start()

    for i, o in enumerate(ORDER):
        if i == FIRST:
            send_codes()
        pr, pc = shift(r, c, o)
        packed[i] = child[picks[0, pr * 4 + pc]]
        landing, recv = (incoming.at[i], tile_recv) if i < EARLY else (incoming_late.at[i - EARLY], late_recv)
        remote(packed.at[i], landing, tile_send, recv, (pr, pc)).start()
    last = len(ORDER)
    code_in[last] = code_rows[me]
    incoming_late[last - EARLY] = child[picks[0, me]]

    wait_bytes(code_in.at[pl.ds(0, last)], code_recv)
    wait_bytes(code_rows.at[pl.ds(0, last)], code_send)
    got = code_in[...].reshape(128, 128)
    down = lax.broadcasted_iota(jnp.int32, (128, 128), 0)
    across = lax.broadcasted_iota(jnp.int32, (128, 128), 1)
    late = (down >= EARLY).astype(jnp.int32)
    place_in = jnp.where(got > 0, (got - 1) // 64, 127)
    group = late * 128 + place_in
    key = group * 128 + down
    smaller = to_rows(key) < key
    rank = jnp.sum(smaller.astype(jnp.int32), axis=1, keepdims=True)
    source = jnp.sum(jnp.where(rank == across, down, 0), axis=0, keepdims=True)
    in_order = jnp.sum(jnp.where(rank == across, group, 0), axis=0, keepdims=True)
    before = jnp.sum(jnp.where(rank + 1 == across, group, 0), axis=0, keepdims=True)
    first = lax.broadcasted_iota(jnp.int32, (1, 128), 1) == 0
    sorted_rows[0:1, :] = source % EARLY
    sorted_rows[1:2, :] = ((in_order != before) | first).astype(jnp.int32)
    for n in range(2):
        up_to = jnp.sum((group <= across + 128 * n).astype(jnp.int32), axis=0, keepdims=True)
        equal = jnp.sum((group == across + 128 * n).astype(jnp.int32), axis=0, keepdims=True)
        sorted_rows[2 + n : 3 + n, :] = jnp.maximum(up_to - 1 - EARLY * n, 0)
        sorted_rows[4 + n : 5 + n, :] = equal
    to_scalars = pltpu.make_async_copy(sorted_rows, order, order_sem)
    to_scalars.start()
    to_scalars.wait()
    front_load.wait()
    diag_load.wait()
    for n in range(2):
        high, low = halves(diag_ref[n])
        diag_parts[n] = jnp.concatenate([high, low, high], axis=0)

    def by_diag(a, n):
        high, low = halves(a)
        return lax.dot_general(
            jnp.concatenate([high, high, low], axis=1),
            diag_parts[n],
            (((1,), (0,)), ((), ())),
            preferred_element_type=F32,
        )

    def sums(buffer, start, count):
        def run(t, total):
            tile = buffer[order[0, t]]
            total = jnp.where(order[1, t] > 0, tile, total + tile)
            summed[t] = total
            return total

        lax.fori_loop(start, start + count, run, jnp.zeros((TILE, TILE), F32))

    def assembled(q, n):
        added = summed.at[pl.ds(EARLY * n, (EARLY, 128 - EARLY)[n])][order[2 + n, q]]
        return field[q] + jnp.where(order[4 + n, q] > 0, added, 0.0)

    wait_bytes(incoming, tile_recv)
    sums(incoming, 0, EARLY)

    @pl.loop(0, 72)
    def _(q):
        field[q] = assembled(q, 0)

    wait_bytes(incoming_late.at[pl.ds(0, last - EARLY)], late_recv)
    sums(incoming_late, EARLY, 128 - EARLY)
    for a in range(3):
        tiles[a] = assembled(a * 24, 1)

    target_col = r % 4
    for j in range(4):
        target_row = (r // 4) * 4 + j
        mine = (target_row == r) & (target_col == c)
        src = tiles.at[:, pl.ds(32 * j, 32), :]

        @pl.when(mine)
        def _():
            pltpu.make_async_copy(src, quarter.at[c], q_recv).start()

        @pl.when(jnp.logical_not(mine))
        def _():
            remote(src, quarter.at[c], q_send, q_recv, (target_row, target_col)).start()

    sends_corner = ((r == 2) | (r == 3)) & (c < 2)

    @pl.when(sends_corner)
    def _():
        for i in range(16):
            src = tiles.at[0, 8 * i : 8 * i + 8, :]
            for tc in range(4):
                dev = (i + 16 * (r - 2), tc)
                copy = remote(src, corner.at[c], c_send, c_recv, dev)
                if i != 2:
                    copy.start()
                    continue
                mine = (r == 2) & (c == tc)

                @pl.when(mine)
                def _():
                    pltpu.make_async_copy(src, corner.at[c], c_recv).start()

                @pl.when(jnp.logical_not(mine))
                def _():
                    copy.start()

    for a in range(3):

        @pl.loop(1, 24)
        def _(b):
            field[a * 24 + b] = assembled(a * 24 + b, 1)

    wait_bytes(quarter, q_recv)
    wait_bytes(corner, c_recv)

    for d in (1, 3, 2):
        remote(tiles, own_ref.at[c], o_send, o_recv, (r, (c + d) % 4)).start()
    own = pltpu.make_async_copy(tiles, own_ref.at[c], own_sem)
    own.start()

    left = jnp.concatenate([quarter[0].reshape(96, TILE), quarter[1].reshape(96, TILE)], axis=1)
    extra = jnp.concatenate([corner[0], corner[1]], axis=1)
    right = jnp.concatenate([quarter[2].reshape(96, TILE), quarter[3].reshape(96, TILE)], axis=1)
    one = by_diag(jnp.concatenate([left, extra], axis=0), 0)
    two = by_diag(right, 1)
    all_ref[pl.ds(r, 1)] = jnp.concatenate([one, two], axis=0).reshape(1, SHARD, 256)

    def shard_row(da, db):
        sx = (x + (1 - k) * da + k * db + 8) % 4
        sz = (z + k * da + (1 - k) * db + 8) % 4
        return sx * 8 + sz * 2 + k

    def piece(da, db, p):
        return all_ref.at[shard_row(da, db), pl.ds(*PIECES[p]), :]

    def pass_on(ref, sem, dev):
        remote(ref, ref, g_send, sem, dev).start()

    twin = (r + 1 - 2 * k, c)
    away = (0, -1, 1, 2)
    count = len(PIECES)
    up = range(count // 2)
    down = range(count // 2, count)

    def to_second(i, p):
        for d in (1, -1) if p in up else (-1, 1):
            sem = second_recv.at[(3 * i + (0 if d == 1 else 1)) * count + p]
            pass_on(piece(away[i], 0, p), sem, (shard_row(0, d), c))

    def came_first(way, p):
        ref = piece(away[way + 1], 0, p)
        wait_bytes(ref, first_recv.at[way * count + p])
        if way == 0 and p in up:
            pass_on(ref, first_recv.at[2 * count + p], (shard_row(1, 0), c))
        if way == 1 and p in down:
            pass_on(ref, first_recv.at[2 * count + p], (shard_row(-1, 0), c))
        to_second(way + 1, p)
        pass_on(ref, twin_recv, twin)

    def came_second(i, way, p):
        ref = piece(away[i], (-1, 1, 2)[way], p)
        wait_bytes(ref, second_recv.at[(3 * i + way) * count + p])
        if way == 0 and p in up:
            pass_on(ref, second_recv.at[(3 * i + 2) * count + p], (shard_row(0, 1), c))
        if way == 1 and p in down:
            pass_on(ref, second_recv.at[(3 * i + 2) * count + p], (shard_row(0, -1), c))
        pass_on(ref, twin_recv, twin)

    passed = [(way, pair[way]) for pair in zip(up, down) for way in (0, 1)]
    kept = [(way, pair[1 - way]) for pair in zip(up, down) for way in (0, 1)]
    for way, p in passed + kept:
        d = 1 - 2 * way
        pass_on(piece(0, 0, p), first_recv.at[way * count + p], (shard_row(d, 0), c))
    for p in range(count):
        to_second(0, p)
    for p in range(count):
        pass_on(piece(0, 0, p), twin_recv, twin)
    for some in (passed, kept):
        for way, p in some:
            came_first(way, p)
        for way, p in some:
            came_second(0, way, p)
    for p in range(count):
        came_first(2, p)
    for p in range(count):
        came_second(0, 2, p)
    for i in (1, 2, 3):
        for way, p in passed + kept:
            came_second(i, way, p)

    for i in (1, 2, 3):
        for p in range(count):
            came_second(i, 2, p)
    own.wait()
    wait_bytes(own_ref.at[pl.ds(0, 3)], o_recv)
    left = jnp.concatenate([own_ref[0].reshape(384, TILE), own_ref[1].reshape(384, TILE)], axis=1)
    right = jnp.concatenate([own_ref[2].reshape(384, TILE), own_ref[3].reshape(384, TILE)], axis=1)
    rows_ref[0] = by_diag(left, 0)
    rows_ref[1] = by_diag(right, 1)
    wait_bytes(all_ref.at[pl.ds(0, 16)], twin_recv)
    wait_bytes(all_ref.at[pl.ds(0, 31)], g_send)
    wait_bytes(own_ref.at[pl.ds(0, 3)], o_send)

    wait_bytes(packed.at[pl.ds(0, last)], tile_send)
    row_quarter = tiles.at[:, pl.ds(0, 32), :]
    holds_one = (r % 4) == c
    for j in range(4):

        @pl.when(jnp.logical_not(holds_one & ((r % 4) == j)))
        def _():
            wait_bytes(row_quarter, q_send)

    @pl.when(sends_corner)
    def _():
        @pl.loop(0, 63)
        def _(n):
            wait_bytes(corner.at[0], c_send)

        @pl.when(r == 3)
        def _():
            wait_bytes(corner.at[0], c_send)


def assemble(count, dest, slot, child, front, diag):
    any_space = pl.BlockSpec(memory_space=pl.ANY)
    vmem = pl.BlockSpec(memory_space=pltpu.VMEM)
    dma = pltpu.SemaphoreType.DMA
    return pl.pallas_call(
        assemble_kernel,
        out_shape=(
            pltpu.VMEM((72, TILE, TILE), F32),
            pltpu.VMEM((32, SHARD, 256), F32),
            pltpu.VMEM((2, 384, 256), F32),
            pltpu.VMEM((2, 256, 256), F32),
        ),
        in_specs=[pl.BlockSpec(memory_space=pltpu.SMEM)] + [any_space] * 5,
        out_specs=(vmem,) * 4,
        scratch_shapes=[
            pltpu.VMEM((1, 64), jnp.int32),
            pltpu.VMEM((1, 64), jnp.int32),
            pltpu.VMEM((64, TILE, TILE), F32),
            pltpu.VMEM((128, TILE, TILE), F32),
            pltpu.VMEM((128, TILE, TILE), F32),
            pltpu.VMEM((EARLY, TILE, TILE), F32),
            pltpu.VMEM((128 - EARLY, TILE, TILE), F32),
            pltpu.VMEM((4, 3, TILE, TILE), F32),
            pltpu.VMEM((2, 768, 256), BF16),
            pltpu.VMEM((128, 1, 128), jnp.int32),
            pltpu.VMEM((128, 1, 128), jnp.int32),
            pltpu.VMEM((8, 128), jnp.int32),
            pltpu.VMEM((8, 128), jnp.int32),
            pltpu.SMEM((8, 128), jnp.int32),
            pltpu.SMEM((8, 128), jnp.int32),
            pltpu.VMEM((3, TILE, TILE), F32),
            pltpu.VMEM((4, 3, 32, TILE), F32),
            pltpu.VMEM((2, 8, TILE), F32),
            pltpu.SemaphoreType.REGULAR,
            pltpu.SemaphoreType.REGULAR,
            dma((2,)),
        ]
        + [dma] * 17
        + [dma((12,)), dma((48,)), dma, dma],
        compiler_params=pltpu.CompilerParams(
            collective_id=0, has_side_effects=True, vmem_limit_bytes=VMEM_LIMIT
        ),
        name="assemble",
    )(count, *[pltpu.with_memory_space_constraint(v, pltpu.HBM) for v in (dest, slot, child, front, diag)])


def update_kernel(field, all_ref, rows_ref, diag_ref, out_hbm, stage, row_parts, panel_ref, out_sem):
    r = lax.axis_index("row")
    c = lax.axis_index("col")
    corner = all_ref[:, 96:104, :].reshape(256, 256)
    both = halves(dot3(corner, diag_ref[1], ((0,), (0,))))
    p_one = rows_ref[0]
    p_two = rows_ref[1] - dot3(p_one, both)
    tile_row = (lax.broadcasted_iota(jnp.int32, (384, 1), 0) // TILE) * 32 + r
    zero = jnp.zeros_like(p_one)
    p_two = jnp.where(tile_row >= 2, p_two, zero)
    panel = jnp.where(
        c < 2,
        jnp.where(c == 0, p_one[:, :TILE], p_one[:, TILE:]),
        jnp.where(c == 2, p_two[:, :TILE], p_two[:, TILE:]),
    )
    panel_ref[...] = panel.reshape(3, TILE, TILE)
    second = jnp.where(tile_row >= 4, p_two, zero)
    first = jnp.where(tile_row >= 2, p_one, zero) - dot3(second, both, ((1,), (1,)))
    high, low = halves(jnp.concatenate([first, second], axis=1))
    row_parts[...] = jnp.concatenate([high, high, low], axis=1)

    @pl.loop(0, 4)
    def _(pair):
        shards = [pl.ds(pl.multiple_of(8 * pair + 4 * n, 4), 4) for n in range(2)]
        both_ways = [
            jnp.concatenate(
                [all_ref[rows, 32 * b + start : 32 * b + start + 32, :].reshape(TILE, 256) for rows in shards for b in range(3)]
            )
            for start in (0, 104)
        ]
        high, low = halves(jnp.concatenate(both_ways, axis=1))
        product = lax.dot_general(
            row_parts[...],
            jnp.concatenate([high, low, high], axis=1),
            (((1,), (1,)), ((), ())),
            preferred_element_type=F32,
        )
        for a in range(3):
            for n in range(2):
                for b in range(3):
                    across = TILE * (3 * n + b)
                    part = product[TILE * a : TILE * a + TILE, across : across + TILE]
                    stage[3 * a + b, 2 * pair + n] = field[3 * a + b, 2 * pair + n] - part

        @pl.when(pair == 0)
        def _():
            for a in range(3):
                stage[3 * a, 0] = panel_ref[a]

        done = pl.ds(2 * pair, 2)
        pltpu.make_async_copy(stage.at[:, done], out_hbm.at[:, done], out_sem).start()

    wait_bytes(stage, out_sem)


def update(field, gathered, rows, diag):
    vmem = pl.BlockSpec(memory_space=pltpu.VMEM)
    shape = (9, 8, TILE, TILE)
    return pl.pallas_call(
        update_kernel,
        out_shape=jax.ShapeDtypeStruct(shape, F32),
        in_specs=[vmem] * 4,
        out_specs=pl.BlockSpec(memory_space=pl.ANY),
        scratch_shapes=[
            pltpu.VMEM(shape, F32),
            pltpu.VMEM((384, 1536), BF16),
            pltpu.VMEM((3, TILE, TILE), F32),
            pltpu.SemaphoreType.DMA,
        ],
        compiler_params=pltpu.CompilerParams(vmem_limit_bytes=VMEM_LIMIT),
        name="update",
    )(field.reshape(shape), gathered, rows, diag)


def body(front, child_tiles, tile_dest, tile_slot, tile_count, diag_inverses):
    field, gathered, rows, diag = assemble(
        tile_count,
        tile_dest.reshape(1, 64),
        tile_slot.reshape(1, 64),
        child_tiles,
        front.reshape(72, TILE, TILE),
        diag_inverses,
    )
    return update(field, gathered, rows, diag).reshape(front.shape)


def solution(mesh):
    return jax.shard_map(
        body,
        mesh=mesh,
        in_specs=(
            P(None, "row", None, "col", None, None),
            P(("row", "col"), None, None),
            P(("row", "col"), None),
            P(("row", "col")),
            P(("row", "col")),
            P(),
        ),
        out_specs=P(None, "row", None, "col", None, None),
        check_vma=False,
    )
```

```python
import itertools

import jax
import jax.numpy as jnp
from jax import lax
from jax.experimental import pallas as pl
from jax.experimental.pallas import tpu as pltpu
from jax.sharding import PartitionSpec as P

MESH = pl.DeviceIdType.MESH
F32 = jnp.float32
BF16 = jnp.bfloat16
VMEM_LIMIT = 40 * 2**20
TILE = 128
FIRST = 12
EARLY = 96
PIECES = ((0, 56), (56, 48), (104, 48), (152, 48))
SHARD = 200


def place(r, c):
    return r // 8, c, (r // 2) % 4, r % 2


def device(x, y, z, k):
    return x * 8 + z * 2 + k, y


def shift(r, c, o):
    x, y, z, k = place(r, c)
    return device((x + o[0]) % 4, (y + o[1]) % 4, (z + o[2]) % 4, (k + o[3]) % 2)


def exchange_order():
    def negated(o):
        return (-o[0]) % 4, (-o[1]) % 4, (-o[2]) % 4, o[3]

    orbits, seen = [], set()
    for o in itertools.product(range(4), range(4), range(4), range(2)):
        if o in seen or o == (0, 0, 0, 0):
            continue
        orbit, a = [], o
        for _ in range(3):
            for b in (a, negated(a)):
                if b not in orbit:
                    orbit.append(b)
            a = (a[1], a[2], a[0], a[3])
        seen |= set(orbit)
        orbits.append(orbit)
    far = sorted(orbits, key=lambda orbit: -sum(min(v, 4 - v) for v in orbit[0][:3]))
    order = []
    while far:
        order += far.pop(0)
        if far:
            order += far.pop(-1)
    return order


ORDER = exchange_order()


def signal(sem, dev):
    pl.semaphore_signal(sem, inc=1, device_id=dev, device_id_type=MESH)


def enter(r, c, line_sem, column_sem):
    barrier = pltpu.get_barrier_semaphore()
    plane = [shift(r, c, (0, 0, dz, dk)) for dz in range(4) for dk in range(2) if dz or dk]
    lines = [shift(r, c, (d, 0, 0, 0)) for d in (1, 2, 3)]
    columns = [shift(r, c, (0, d, 0, 0)) for d in (1, 2, 3)]
    for dev in plane + lines + columns:
        signal(barrier, dev)
    pl.semaphore_wait(barrier, 13)
    for dev in lines:
        signal(line_sem, dev)
    pl.semaphore_wait(line_sem, 3)
    for dev in columns:
        signal(column_sem, dev)
    pl.semaphore_wait(column_sem, 3)


def remote(src, dst, send, recv, dev):
    return pltpu.make_async_remote_copy(
        src_ref=src, dst_ref=dst, send_sem=send, recv_sem=recv, device_id=dev, device_id_type=MESH
    )


def wait_bytes(ref, sem):
    pltpu.make_async_copy(ref, ref, sem).wait()


def halves(a):
    high = a.astype(BF16)
    return high, (a - high.astype(F32)).astype(BF16)


def dot3(a, b, dims=((1,), (0,))):
    ah, al = a if isinstance(a, tuple) else halves(a)
    bh, bl = b if isinstance(b, tuple) else halves(b)

    (da,), (db,) = dims
    return lax.dot_general(
        jnp.concatenate([ah, ah, al], axis=da),
        jnp.concatenate([bh, bl, bh], axis=db),
        (dims, ((), ())),
        preferred_element_type=F32,
    )


def to_rows(column):
    down = lax.broadcasted_iota(jnp.int32, (128, 128), 0)
    across = lax.broadcasted_iota(jnp.int32, (128, 128), 1)
    return jnp.sum(jnp.where(down == across, column, 0), axis=0, keepdims=True)


def assemble_kernel(
    count_ref,
    dest_hbm,
    slot_hbm,
    child_hbm,
    front_hbm,
    diag_hbm,
    field,
    all_ref,
    rows_ref,
    diag_ref,
    dest_ref,
    slot_ref,
    child,
    packed,
    summed,
    incoming,
    incoming_late,
    own_ref,
    diag_parts,
    code_rows,
    code_in,
    rows,
    sorted_rows,
    picks,
    order,
    tiles,
    quarter,
    corner,
    line_sem,
    column_sem,
    small_sem,
    child_sem,
    front_sem,
    diag_sem,
    rows_sem,
    order_sem,
    tile_send,
    tile_recv,
    late_recv,
    code_send,
    code_recv,
    own_sem,
    q_send,
    q_recv,
    c_send,
    c_recv,
    o_send,
    o_recv,
    first_recv,
    second_recv,
    twin_recv,
    g_send,
):
    r = lax.axis_index("row")
    c = lax.axis_index("col")
    x, _, z, k = place(r, c)
    me = r * 4 + c
    loads = [
        pltpu.make_async_copy(dest_hbm, dest_ref, small_sem.at[0]),
        pltpu.make_async_copy(slot_hbm, slot_ref, small_sem.at[1]),
    ]
    for load in loads:
        load.start()
    child_load = pltpu.make_async_copy(child_hbm, child, child_sem)
    child_load.start()
    front_load = pltpu.make_async_copy(front_hbm, field, front_sem)
    front_load.start()
    diag_load = pltpu.make_async_copy(diag_hbm, diag_ref, diag_sem)
    diag_load.start()
    for load in loads:
        load.wait()

    down = lax.broadcasted_iota(jnp.int32, (128, 64), 0)
    slot = lax.broadcasted_iota(jnp.int32, (128, 64), 1)
    hits = (dest_ref[...] == down) & (slot < count_ref[0])
    code = jnp.sum(jnp.where(hits, slot_ref[...] * 64 + slot + 1, 0), axis=1, keepdims=True)
    code = jnp.broadcast_to(code, (128, 128))
    code_rows[...] = code.reshape(128, 1, 128)
    rows[0:1, :] = jnp.maximum(to_rows(code) - 1, 0) % 64
    to_scalars = pltpu.make_async_copy(rows, picks, rows_sem)
    to_scalars.start()
    enter(r, c, line_sem, column_sem)
    to_scalars.wait()
    child_load.wait()

    def send_codes():
        for i, o in enumerate(ORDER):
            pr, pc = shift(r, c, o)
            remote(code_rows.at[pr * 4 + pc], code_in.at[i], code_send, code_recv, (pr, pc)).start()

    for i, o in enumerate(ORDER):
        if i == FIRST:
            send_codes()
        pr, pc = shift(r, c, o)
        packed[i] = child[picks[0, pr * 4 + pc]]
        landing, recv = (incoming.at[i], tile_recv) if i < EARLY else (incoming_late.at[i - EARLY], late_recv)
        remote(packed.at[i], landing, tile_send, recv, (pr, pc)).start()
    last = len(ORDER)
    code_in[last] = code_rows[me]
    incoming_late[last - EARLY] = child[picks[0, me]]

    wait_bytes(code_in.at[pl.ds(0, last)], code_recv)
    wait_bytes(code_rows.at[pl.ds(0, last)], code_send)
    got = code_in[...].reshape(128, 128)
    down = lax.broadcasted_iota(jnp.int32, (128, 128), 0)
    across = lax.broadcasted_iota(jnp.int32, (128, 128), 1)
    late = (down >= EARLY).astype(jnp.int32)
    place_in = jnp.where(got > 0, (got - 1) // 64, 127)
    group = late * 128 + place_in
    key = group * 128 + down
    smaller = to_rows(key) < key
    rank = jnp.sum(smaller.astype(jnp.int32), axis=1, keepdims=True)
    source = jnp.sum(jnp.where(rank == across, down, 0), axis=0, keepdims=True)
    in_order = jnp.sum(jnp.where(rank == across, group, 0), axis=0, keepdims=True)
    before = jnp.sum(jnp.where(rank + 1 == across, group, 0), axis=0, keepdims=True)
    first = lax.broadcasted_iota(jnp.int32, (1, 128), 1) == 0
    sorted_rows[0:1, :] = source % EARLY
    sorted_rows[1:2, :] = ((in_order != before) | first).astype(jnp.int32)
    for n in range(2):
        up_to = jnp.sum((group <= across + 128 * n).astype(jnp.int32), axis=0, keepdims=True)
        equal = jnp.sum((group == across + 128 * n).astype(jnp.int32), axis=0, keepdims=True)
        sorted_rows[2 + n : 3 + n, :] = jnp.maximum(up_to - 1 - EARLY * n, 0)
        sorted_rows[4 + n : 5 + n, :] = equal
    to_scalars = pltpu.make_async_copy(sorted_rows, order, order_sem)
    to_scalars.start()
    to_scalars.wait()
    front_load.wait()
    diag_load.wait()
    for n in range(2):
        high, low = halves(diag_ref[n])
        diag_parts[n] = jnp.concatenate([high, low, high], axis=0)

    def by_diag(a, n):
        high, low = halves(a)
        return lax.dot_general(
            jnp.concatenate([high, high, low], axis=1),
            diag_parts[n],
            (((1,), (0,)), ((), ())),
            preferred_element_type=F32,
        )

    def sums(buffer, start, count):
        def run(t, total):
            tile = buffer[order[0, t]]
            total = jnp.where(order[1, t] > 0, tile, total + tile)
            summed[t] = total
            return total

        lax.fori_loop(start, start + count, run, jnp.zeros((TILE, TILE), F32))

    def assembled(q, n):
        added = summed.at[pl.ds(EARLY * n, (EARLY, 128 - EARLY)[n])][order[2 + n, q]]
        return field[q] + jnp.where(order[4 + n, q] > 0, added, 0.0)

    wait_bytes(incoming, tile_recv)
    sums(incoming, 0, EARLY)

    @pl.loop(0, 72)
    def _(q):
        field[q] = assembled(q, 0)

    wait_bytes(incoming_late.at[pl.ds(0, last - EARLY)], late_recv)
    sums(incoming_late, EARLY, 128 - EARLY)
    for a in range(3):
        tiles[a] = assembled(a * 24, 1)

    target_col = r % 4
    for j in range(4):
        target_row = (r // 4) * 4 + j
        mine = (target_row == r) & (target_col == c)
        src = tiles.at[:, pl.ds(32 * j, 32), :]

        @pl.when(mine)
        def _():
            pltpu.make_async_copy(src, quarter.at[c], q_recv).start()

        @pl.when(jnp.logical_not(mine))
        def _():
            remote(src, quarter.at[c], q_send, q_recv, (target_row, target_col)).start()

    sends_corner = ((r == 2) | (r == 3)) & (c < 2)

    @pl.when(sends_corner)
    def _():
        for i in range(16):
            src = tiles.at[0, 8 * i : 8 * i + 8, :]
            for tc in range(4):
                dev = (i + 16 * (r - 2), tc)
                copy = remote(src, corner.at[c], c_send, c_recv, dev)
                if i != 2:
                    copy.start()
                    continue
                mine = (r == 2) & (c == tc)

                @pl.when(mine)
                def _():
                    pltpu.make_async_copy(src, corner.at[c], c_recv).start()

                @pl.when(jnp.logical_not(mine))
                def _():
                    copy.start()

    for a in range(3):

        @pl.loop(1, 24)
        def _(b):
            field[a * 24 + b] = assembled(a * 24 + b, 1)

    wait_bytes(quarter, q_recv)
    wait_bytes(corner, c_recv)

    for d in (1, 3, 2):
        remote(tiles, own_ref.at[c], o_send, o_recv, (r, (c + d) % 4)).start()
    own = pltpu.make_async_copy(tiles, own_ref.at[c], own_sem)
    own.start()

    left = jnp.concatenate([quarter[0].reshape(96, TILE), quarter[1].reshape(96, TILE)], axis=1)
    extra = jnp.concatenate([corner[0], corner[1]], axis=1)
    right = jnp.concatenate([quarter[2].reshape(96, TILE), quarter[3].reshape(96, TILE)], axis=1)
    one = by_diag(jnp.concatenate([left, extra], axis=0), 0)
    two = by_diag(right, 1)
    all_ref[pl.ds(r, 1)] = jnp.concatenate([one, two], axis=0).reshape(1, SHARD, 256)

    def shard_row(da, db):
        sx = (x + (1 - k) * da + k * db + 8) % 4
        sz = (z + k * da + (1 - k) * db + 8) % 4
        return sx * 8 + sz * 2 + k

    def piece(da, db, p):
        return all_ref.at[shard_row(da, db), pl.ds(*PIECES[p]), :]

    def pass_on(ref, sem, dev):
        remote(ref, ref, g_send, sem, dev).start()

    twin = (r + 1 - 2 * k, c)
    away = (0, -1, 1, 2)
    count = len(PIECES)
    up = range(count // 2)
    down = range(count // 2, count)

    def to_second(i, p):
        for d in (1, -1) if p in up else (-1, 1):
            sem = second_recv.at[(3 * i + (0 if d == 1 else 1)) * count + p]
            pass_on(piece(away[i], 0, p), sem, (shard_row(0, d), c))

    def came_first(way, p):
        ref = piece(away[way + 1], 0, p)
        wait_bytes(ref, first_recv.at[way * count + p])
        if way == 0 and p in up:
            pass_on(ref, first_recv.at[2 * count + p], (shard_row(1, 0), c))
        if way == 1 and p in down:
            pass_on(ref, first_recv.at[2 * count + p], (shard_row(-1, 0), c))
        to_second(way + 1, p)
        pass_on(ref, twin_recv, twin)

    def came_second(i, way, p):
        ref = piece(away[i], (-1, 1, 2)[way], p)
        wait_bytes(ref, second_recv.at[(3 * i + way) * count + p])
        if way == 0 and p in up:
            pass_on(ref, second_recv.at[(3 * i + 2) * count + p], (shard_row(0, 1), c))
        if way == 1 and p in down:
            pass_on(ref, second_recv.at[(3 * i + 2) * count + p], (shard_row(0, -1), c))
        pass_on(ref, twin_recv, twin)

    passed = [(way, pair[way]) for pair in zip(up, down) for way in (0, 1)]
    kept = [(way, pair[1 - way]) for pair in zip(up, down) for way in (0, 1)]
    for way, p in passed + kept:
        d = 1 - 2 * way
        pass_on(piece(0, 0, p), first_recv.at[way * count + p], (shard_row(d, 0), c))
    for p in range(count):
        to_second(0, p)
    for p in range(count):
        pass_on(piece(0, 0, p), twin_recv, twin)
    for some in (passed, kept):
        for way, p in some:
            came_first(way, p)
        for way, p in some:
            came_second(0, way, p)
    for p in range(count):
        came_first(2, p)
    for p in range(count):
        came_second(0, 2, p)
    for i in (1, 2, 3):
        for way, p in passed + kept:
            came_second(i, way, p)

    for i in (1, 2, 3):
        for p in range(count):
            came_second(i, 2, p)
    own.wait()
    wait_bytes(own_ref.at[pl.ds(0, 3)], o_recv)
    left = jnp.concatenate([own_ref[0].reshape(384, TILE), own_ref[1].reshape(384, TILE)], axis=1)
    right = jnp.concatenate([own_ref[2].reshape(384, TILE), own_ref[3].reshape(384, TILE)], axis=1)
    rows_ref[0] = by_diag(left, 0)
    rows_ref[1] = by_diag(right, 1)
    wait_bytes(all_ref.at[pl.ds(0, 16)], twin_recv)
    wait_bytes(all_ref.at[pl.ds(0, 31)], g_send)
    wait_bytes(own_ref.at[pl.ds(0, 3)], o_send)

    wait_bytes(packed.at[pl.ds(0, last)], tile_send)
    row_quarter = tiles.at[:, pl.ds(0, 32), :]
    holds_one = (r % 4) == c
    for j in range(4):

        @pl.when(jnp.logical_not(holds_one & ((r % 4) == j)))
        def _():
            wait_bytes(row_quarter, q_send)

    @pl.when(sends_corner)
    def _():
        @pl.loop(0, 63)
        def _(n):
            wait_bytes(corner.at[0], c_send)

        @pl.when(r == 3)
        def _():
            wait_bytes(corner.at[0], c_send)


def assemble(count, dest, slot, child, front, diag):
    any_space = pl.BlockSpec(memory_space=pl.ANY)
    vmem = pl.BlockSpec(memory_space=pltpu.VMEM)
    dma = pltpu.SemaphoreType.DMA
    return pl.pallas_call(
        assemble_kernel,
        out_shape=(
            pltpu.VMEM((72, TILE, TILE), F32),
            pltpu.VMEM((32, SHARD, 256), F32),
            pltpu.VMEM((2, 384, 256), F32),
            pltpu.VMEM((2, 256, 256), F32),
        ),
        in_specs=[pl.BlockSpec(memory_space=pltpu.SMEM)] + [any_space] * 5,
        out_specs=(vmem,) * 4,
        scratch_shapes=[
            pltpu.VMEM((1, 64), jnp.int32),
            pltpu.VMEM((1, 64), jnp.int32),
            pltpu.VMEM((64, TILE, TILE), F32),
            pltpu.VMEM((128, TILE, TILE), F32),
            pltpu.VMEM((128, TILE, TILE), F32),
            pltpu.VMEM((EARLY, TILE, TILE), F32),
            pltpu.VMEM((128 - EARLY, TILE, TILE), F32),
            pltpu.VMEM((4, 3, TILE, TILE), F32),
            pltpu.VMEM((2, 768, 256), BF16),
            pltpu.VMEM((128, 1, 128), jnp.int32),
            pltpu.VMEM((128, 1, 128), jnp.int32),
            pltpu.VMEM((8, 128), jnp.int32),
            pltpu.VMEM((8, 128), jnp.int32),
            pltpu.SMEM((8, 128), jnp.int32),
            pltpu.SMEM((8, 128), jnp.int32),
            pltpu.VMEM((3, TILE, TILE), F32),
            pltpu.VMEM((4, 3, 32, TILE), F32),
            pltpu.VMEM((2, 8, TILE), F32),
            pltpu.SemaphoreType.REGULAR,
            pltpu.SemaphoreType.REGULAR,
            dma((2,)),
        ]
        + [dma] * 17
        + [dma((12,)), dma((48,)), dma, dma],
        compiler_params=pltpu.CompilerParams(
            collective_id=0, has_side_effects=True, vmem_limit_bytes=VMEM_LIMIT
        ),
        name="assemble",
    )(count, *[pltpu.with_memory_space_constraint(v, pltpu.HBM) for v in (dest, slot, child, front, diag)])


def update_kernel(field, all_ref, rows_ref, diag_ref, out_hbm, stage, row_parts, panel_ref, out_sem):
    r = lax.axis_index("row")
    c = lax.axis_index("col")
    corner = all_ref[:, 96:104, :].reshape(256, 256)
    both = halves(dot3(corner, diag_ref[1], ((0,), (0,))))
    p_one = rows_ref[0]
    p_two = rows_ref[1] - dot3(p_one, both)
    tile_row = (lax.broadcasted_iota(jnp.int32, (384, 1), 0) // TILE) * 32 + r
    zero = jnp.zeros_like(p_one)
    p_two = jnp.where(tile_row >= 2, p_two, zero)
    panel = jnp.where(
        c < 2,
        jnp.where(c == 0, p_one[:, :TILE], p_one[:, TILE:]),
        jnp.where(c == 2, p_two[:, :TILE], p_two[:, TILE:]),
    )
    panel_ref[...] = panel.reshape(3, TILE, TILE)
    second = jnp.where(tile_row >= 4, p_two, zero)
    first = jnp.where(tile_row >= 2, p_one, zero) - dot3(second, both, ((1,), (1,)))
    high, low = halves(jnp.concatenate([first, second], axis=1))
    row_parts[...] = jnp.concatenate([high, high, low], axis=1)

    @pl.loop(0, 4)
    def _(pair):
        shards = [pl.ds(pl.multiple_of(8 * pair + 4 * n, 4), 4) for n in range(2)]
        both_ways = [
            jnp.concatenate(
                [all_ref[rows, 32 * b + start : 32 * b + start + 32, :].reshape(TILE, 256) for rows in shards for b in range(3)]
            )
            for start in (0, 104)
        ]
        high, low = halves(jnp.concatenate(both_ways, axis=1))
        product = lax.dot_general(
            row_parts[...],
            jnp.concatenate([high, low, high], axis=1),
            (((1,), (1,)), ((), ())),
            preferred_element_type=F32,
        )
        for a in range(3):
            for n in range(2):
                for b in range(3):
                    across = TILE * (3 * n + b)
                    part = product[TILE * a : TILE * a + TILE, across : across + TILE]
                    stage[3 * a + b, 2 * pair + n] = field[3 * a + b, 2 * pair + n] - part

        @pl.when(pair == 0)
        def _():
            for a in range(3):
                stage[3 * a, 0] = panel_ref[a]

        done = pl.ds(2 * pair, 2)
        pltpu.make_async_copy(stage.at[:, done], out_hbm.at[:, done], out_sem).start()

    wait_bytes(stage, out_sem)


def update(field, gathered, rows, diag):
    vmem = pl.BlockSpec(memory_space=pltpu.VMEM)
    shape = (9, 8, TILE, TILE)
    return pl.pallas_call(
        update_kernel,
        out_shape=jax.ShapeDtypeStruct(shape, F32),
        in_specs=[vmem] * 4,
        out_specs=pl.BlockSpec(memory_space=pl.ANY),
        scratch_shapes=[
            pltpu.VMEM(shape, F32),
            pltpu.VMEM((384, 1536), BF16),
            pltpu.VMEM((3, TILE, TILE), F32),
            pltpu.SemaphoreType.DMA,
        ],
        compiler_params=pltpu.CompilerParams(vmem_limit_bytes=VMEM_LIMIT),
        name="update",
    )(field.reshape(shape), gathered, rows, diag)


def body(front, child_tiles, tile_dest, tile_slot, tile_count, diag_inverses):
    field, gathered, rows, diag = assemble(
        tile_count,
        tile_dest.reshape(1, 64),
        tile_slot.reshape(1, 64),
        child_tiles,
        front.reshape(72, TILE, TILE),
        diag_inverses,
    )
    return update(field, gathered, rows, diag).reshape(front.shape)


def solution(mesh):
    return jax.shard_map(
        body,
        mesh=mesh,
        in_specs=(
            P(None, "row", None, "col", None, None),
            P(("row", "col"), None, None),
            P(("row", "col"), None),
            P(("row", "col")),
            P(("row", "col")),
            P(),
        ),
        out_specs=P(None, "row", None, "col", None, None),
        check_vma=False,
    )
```
